128 devices in a mesh: band: 4 (over y_lo, core), tile: 32 (over y_hi, z, x).
Axes of the slice: x: 4, y: 4 (y_hi: 2, y_lo: 2; y = y_hi * 2 + y_lo), z: 4, core: 2. Of those that a mesh axis runs over, the one named last changes fastest.
Arguments:
- cond_x: float32 [8, 2048, 2048], P('band', 'tile'), may hold values from 0.2 to 5
- cond_y: float32 [8, 2048, 2048], P('band', 'tile'), may hold values from 0.2 to 5
- via_cond: float32 [8, 2048, 2048], P('band', 'tile'), may hold values from 0.5 to 8
- via_mask: int32 [8, 2048, 2048], P('band', 'tile'), may hold values 0 or 1
- capacitance: float32 [8, 2048, 2048], P('band', 'tile'), may hold values from 0.5 to 4
- pad_mask: int32 [8, 2048, 2048], P('band', 'tile'), may hold values 0 or 1
- observe: float32 [2, 8, 2048, 2048], P(None, 'band', 'tile'), may hold values from -40 to 40
Outputs:
- adjoint: float32 [2, 8, 2048, 2048], P(None, 'band', 'tile')
The draws below stay inside these ranges and needn't reach their ends.
All inputs are finite; a program needn't handle non-finite values. No bound on the sum of `via_mask` or of `pad_mask` on one device may be relied on, other than what follows from the above.
Results may differ from the reference program's by a relative error of at most 0.0003.
Values sent between devices are 32-bit elements; how exact they have to be, the bound alone decides.
A program may use at most 128 MiB of HBM per device.

```python
import math
import jax
import jax.numpy as jnp

NB = 8
NY = 2048
STEPS = 2
ITERS = 2
NX = 2048


def draw_observe(key, part):
    first_key = jax.random.fold_in(key, 0)
    shape = (STEPS, NB, NX, NY)
    rows = jnp.arange(NX, dtype=jnp.float32) / max(NX - 1, 1)
    ramp = (1.0 + 2.0 * rows)[None, None, :, None]
    base = jnp.clip(jax.random.normal(first_key, shape, jnp.float32), -4.0, 4.0)
    return base * ramp


def place_ends(result, stream_key, low, high):
    index_at = [jax.random.randint(jax.random.fold_in(stream_key, axis), (), 0, length) for axis, length in enumerate(result.shape)]
    widest = result.shape.index(max(result.shape))
    neighbour = index_at[:widest] + [(index_at[widest] + 1) % result.shape[widest]] + index_at[widest + 1:]
    return result.at[tuple(index_at)].set(low).at[tuple(neighbour)].set(high)


def level_of(own_key, extent, pieces, low, largest):
    def one(axis_at, blocks):
        draws = jax.random.uniform(jax.random.fold_in(jax.random.fold_in(own_key, 6), axis_at), (blocks,), jnp.float32, low / len(pieces), largest / len(pieces))
        return jnp.repeat(jnp.exp(draws), extent[axis_at] // blocks).reshape((-1,) + (1,) * (len(extent) - axis_at - 1))

    level = one(*pieces[0])
    for cut in pieces[1:]:
        level = level * one(*cut)
    return level


def setup_inputs(seed: int = 0) -> dict:
    arg_keys = jax.random.split(jax.random.key(seed), 8)
    return {
        "cond_x": jnp.clip(jnp.exp(math.log(5.0) - 3.218876 * jax.random.uniform(arg_keys[0], (NB, NX, NY), jnp.float32) ** level_of(arg_keys[0], (NB, NX, NY), ((0, 4), (1, 32)), -0.2, 0.2)), 0.2, 5.0),
        "cond_y": jnp.clip(jnp.exp(math.log(5.0) - 3.218876 * jax.random.uniform(arg_keys[1], (NB, NX, NY), jnp.float32) ** level_of(arg_keys[1], (NB, NX, NY), ((0, 4), (1, 32)), -0.2, 0.2)), 0.2, 5.0),
        "via_cond": jnp.clip(jnp.exp(math.log(8.0) - 2.7725887 * jax.random.uniform(arg_keys[2], (NB, NX, NY), jnp.float32) ** level_of(arg_keys[2], (NB, NX, NY), ((0, 4), (1, 32)), -0.2, 0.2)), 0.5, 8.0),
        "via_mask": place_ends((jax.random.randint(arg_keys[3], (NB, NX, NY), 0, 4) < 1).astype(jnp.int32), jax.random.fold_in(arg_keys[3], 1), 0, 1),
        "capacitance": jnp.clip(jnp.exp(math.log(4.0) - 2.0794415 * jax.random.uniform(arg_keys[4], (NB, NX, NY), jnp.float32) ** level_of(arg_keys[4], (NB, NX, NY), ((0, 4), (1, 32)), -0.2, 0.2)), 0.5, 4.0),
        "pad_mask": place_ends((jax.random.randint(arg_keys[5], (NB, NX, NY), 0, 16) < 1).astype(jnp.int32), jax.random.fold_in(arg_keys[5], 1), 0, 1),
        "observe": draw_observe(jax.random.fold_in(arg_keys[7], 71), 0),
    }


pad_conductance = 4.0


def apply_operator(padded, rims_coeff, diagonal):
    center = padded[1:-1, 1:-1, 1:-1]
    here = rims_coeff[:, 1:-1, 1:-1, 1:-1]
    total = diagonal * center
    total = total + here[0] * (center - padded[1:-1, 2:, 1:-1]) + rims_coeff[0, 1:-1, :-2, 1:-1] * (center - padded[1:-1, :-2, 1:-1])
    total = total + here[1] * (center - padded[1:-1, 1:-1, 2:]) + rims_coeff[1, 1:-1, 1:-1, :-2] * (center - padded[1:-1, 1:-1, :-2])
    total = total + here[2] * (center - padded[2:, 1:-1, 1:-1]) + rims_coeff[2, :-2, 1:-1, 1:-1] * (center - padded[:-2, 1:-1, 1:-1])
    return total


def jacobi_scale(rims_coeff, diagonal):
    here = rims_coeff[:, 1:-1, 1:-1, 1:-1]
    return (diagonal + here[0] + here[1] + here[2] + rims_coeff[0, 1:-1, :-2, 1:-1]
            + rims_coeff[1, 1:-1, 1:-1, :-2] + rims_coeff[2, :-2, 1:-1, 1:-1])


def solve_pcg(right_side, start, operator_fn, scale):
    residual = right_side - operator_fn(start)
    search = residual / scale
    norm_now = jnp.sum(residual * search)
    answer = start
    for iteration in range(ITERS):
        image_vec = operator_fn(search)
        step_len = norm_now / jnp.sum(search * image_vec)
        answer = answer + step_len * search
        residual = residual - step_len * image_vec
        if iteration + 1 < ITERS:
            precond_res = residual / scale
            norm_next = jnp.sum(residual * precond_res)
            search = precond_res + (norm_next / norm_now) * search
            norm_now = norm_next
    return answer


def reference(cond_x, cond_y, via_cond, via_mask, capacitance, pad_mask, observe):
    keep = (jnp.arange(NB) < NB - 1).astype(jnp.float32)[:, None, None]
    via_g = via_cond * via_mask.astype(jnp.float32) * keep
    coeffs = jnp.stack([cond_x, cond_y, via_g])
    rims_coeff = jnp.pad(coeffs, ((0, 0), (1, 1), (1, 1), (1, 1)))
    diagonal = capacitance + pad_conductance * pad_mask.astype(jnp.float32)
    scale = jacobi_scale(rims_coeff, diagonal)

    def operator_fn(values):
        return apply_operator(jnp.pad(values, 1), rims_coeff, diagonal)

    later = jnp.zeros_like(capacitance)
    results = [later] * STEPS
    for time_step in range(STEPS - 1, -1, -1):
        right_side = capacitance * later + observe[time_step]
        if time_step == STEPS - 1:
            start = right_side / scale
        else:
            start = later
        later = solve_pcg(right_side, start, operator_fn, scale)
        results[time_step] = later
    return jnp.stack(results)
```

```python
import functools

import jax
import jax.numpy as jnp
from jax import lax
from jax.experimental import pallas as pl
from jax.experimental.pallas import tpu as pltpu
from jax.sharding import PartitionSpec as P

MESH = pl.DeviceIdType.MESH
PAD_CONDUCTANCE = 4.0
NB = 8
TY, TZ, TX = 2, 4, 4
CH = 8
TOP = 8
X0, Z0, U0, Z1, U1 = range(5)
CX = 5


def lane_sum(p):
    parts = [p[:, k : k + 128] for k in range(0, p.shape[1], 128)]
    while len(parts) > 1:
        parts = [a + b for a, b in zip(parts[::2], parts[1::2])]
    return parts[0]


def kernel(
    cx_hbm, cy_hbm, vc_hbm, vm_hbm, cap_hbm, pm_hbm, ob_hbm, out_hbm,
    cx, cy, vc, vm, cap, pm, ob, vg, cxm, dg, rd, qq, field, halo, below, es, er, acc, ars, arr, adj,
    in_sem, out_sem, ps, pr, gs, gr, ess, ers, ars_sem, arr_sem,
):
    bands = lax.axis_size("band")
    tiles = lax.axis_size("tile")
    band = lax.axis_index("band")
    tile = lax.axis_index("tile")
    rows, cols = cy.shape[1], cy.shape[2]
    n_ch = rows // CH
    has_dn, has_up = band > 0, band < bands - 1
    has_prev, has_next = tile > 0, tile < tiles - 1

    def loads():
        pairs = [
            (vc_hbm, vc), (vm_hbm, vm), (cx_hbm, cx.at[:, pl.ds(TOP, rows), :]), (cy_hbm, cy), (cap_hbm, cap), (pm_hbm, pm),
            (ob_hbm.at[1], ob.at[1]), (ob_hbm.at[0], ob.at[0]),
        ]
        return [pltpu.make_async_copy(s, d, in_sem.at[k]) for k, (s, d) in enumerate(pairs)]

    ld = loads()
    for copy in ld:
        copy.start()

    tx = lax.rem(tile, TX)
    tz = lax.rem(lax.div(tile, TX), TZ)
    ty = lax.div(tile, TX * TZ)

    def peers(stage):
        if stage == 0:
            return [(band, tile - tx + lax.rem(tx + d, TX)) for d in range(1, TX)]
        if stage == 1:
            return [(band, tile + (lax.rem(tz + d, TZ) - tz) * TX) for d in range(1, TZ)]
        both = ty * bands + band
        out = []
        for d in range(1, TY * bands):
            other = lax.rem(both + d, TY * bands)
            out.append((lax.rem(other, bands), tile + (lax.div(other, bands) - ty) * (TX * TZ)))
        return out

    def dev(b, t):
        return {"band": b, "tile": t}

    barrier = pltpu.get_barrier_semaphore()
    known = [p for stage in range(3) for p in peers(stage)]
    known += [(band, lax.rem(tile + 1, tiles)), (band, lax.rem(tile + tiles - 1, tiles))]
    for b, t in known:
        pl.semaphore_signal(barrier, inc=1, device_id=dev(b, t), device_id_type=MESH)

    zero_row = jnp.zeros((1, cols), jnp.float32)
    for f in range(5):
        for b in range(2):
            field[f, b, TOP - 1 : TOP, :] = zero_row
            field[f, b, TOP + rows : TOP + rows + 1, :] = zero_row

    @pl.when(jnp.logical_not(has_dn))
    def _():
        below[...] = jnp.zeros_like(below)

        @pl.loop(0, 5)
        def _(f):
            halo[f, 0] = jnp.zeros((rows, cols), jnp.float32)

    @pl.when(jnp.logical_not(has_up))
    def _():
        @pl.loop(0, 5)
        def _(f):
            halo[f, 1] = jnp.zeros((rows, cols), jnp.float32)

    acc[...] = jnp.zeros_like(acc)

    def ch(c):
        return pl.ds(pl.multiple_of(c * CH, CH), CH)

    def fch(c):
        return pl.ds(pl.multiple_of(TOP + c * CH, CH), CH)

    lane = lax.broadcasted_iota(jnp.int32, (CH, cols), 1)
    sub = lax.broadcasted_iota(jnp.int32, (CH, cols), 0)

    def row_after(here, after):
        return pltpu.roll(jnp.where(sub == 0, after, here), CH - 1, 0)

    def row_before(here, before):
        return pltpu.roll(jnp.where(sub == CH - 1, before, here), 1, 0)

    def plane_copy(f, way, c):
        return pltpu.make_async_remote_copy(
            src_ref=field.at[f, 1 - way, fch(c), :],
            dst_ref=halo.at[f, way, ch(c), :],
            send_sem=ps.at[f, way, c],
            recv_sem=pr.at[f, way, c],
            device_id=dev(band + 1 - 2 * way, tile),
            device_id_type=MESH,
        )

    def via_copy(c):
        return pltpu.make_async_remote_copy(
            src_ref=vg.at[1, ch(c), :],
            dst_ref=below.at[ch(c), :],
            send_sem=gs.at[c],
            recv_sem=gr.at[c],
            device_id=dev(band + 1, tile),
            device_id_type=MESH,
        )

    def edge_copy(f, way):
        return pltpu.make_async_remote_copy(
            src_ref=es.at[f, way],
            dst_ref=er.at[f, way],
            send_sem=ess.at[f, way],
            recv_sem=ers.at[f, way],
            device_id=dev(band, tile + 1 - 2 * way),
            device_id_type=MESH,
        )

    def send_edges(f, i, ways=(0, 1)):
        if 1 in ways:
            @pl.when(jnp.logical_and(i == 0, has_prev))
            def _():
                for b in range(2):
                    es[f, 1, b : b + 1, :] = field[f, b, TOP : TOP + 1, :]
                edge_copy(f, 1).start()
        if 0 in ways:
            @pl.when(jnp.logical_and(i == 1, has_next))
            def _():
                for b in range(2):
                    es[f, 0, b : b + 1, :] = field[f, b, TOP + rows - 1 : TOP + rows, :]
                edge_copy(f, 0).start()

    def take_edges(f, i, ways=(0, 1)):
        if 0 in ways:
            @pl.when(jnp.logical_and(i == 0, has_prev))
            def _():
                edge_copy(f, 0).wait_recv()
                for b in range(2):
                    field[f, b, TOP - 1 : TOP, :] = er[f, 0, b : b + 1, :]
        if 1 in ways:
            @pl.when(jnp.logical_and(i == 1, has_next))
            def _():
                edge_copy(f, 1).wait_recv()
                for b in range(2):
                    field[f, b, TOP + rows : TOP + rows + 1, :] = er[f, 1, b : b + 1, :]

    def send_planes(f, c, ways=(0, 1)):
        for way in ways:
            @pl.when(has_dn if way else has_up)
            def _():
                plane_copy(f, way, c).start()

    def take_planes(f, c, ways=(0, 1)):
        for way in ways:
            @pl.when(has_up if way else has_dn)
            def _():
                plane_copy(f, way, c).wait_recv()

    def order(i):
        return lax.rem(i * (n_ch - 1), n_ch)

    ld[0].wait()
    ld[1].wait()
    pl.semaphore_wait(barrier, len(known))

    @pl.loop(0, n_ch)
    def _(i):
        c = order(i)
        for b in range(2):
            keep = (band * 2 + b < NB - 1).astype(jnp.float32)
            vg[b, ch(c), :] = vc[b, ch(c), :] * vm[b, ch(c), :].astype(jnp.float32) * keep

        @pl.when(has_up)
        def _():
            via_copy(c).start()

    ld[2].wait()

    @pl.when(has_next)
    def _():
        for b in range(2):
            es[CX, 0, b : b + 1, :] = cx[b, TOP + rows - 1 : TOP + rows, :]
        edge_copy(CX, 0).start()

    for b in range(2):
        cx[b, TOP - 1 : TOP, :] = zero_row
    for copy in ld[3:7]:
        copy.wait()

    @pl.when(has_prev)
    def _():
        edge_copy(CX, 0).wait_recv()
        for b in range(2):
            cx[b, TOP - 1 : TOP, :] = er[CX, 0, b : b + 1, :]

    @pl.loop(0, n_ch)
    def _(i):
        c = order(i)

        @pl.when(has_dn)
        def _():
            via_copy(c).wait_recv()

        for b in range(2):
            y_all = cy[b, ch(c), :]
            y_in = jnp.where(lane == cols - 1, 0.0, y_all)
            lower = below[ch(c), :] if b == 0 else vg[0, ch(c), :]
            x_here = cx[b, fch(c), :]
            x_prev = row_before(x_here, cx[b, fch(c - 1), :])
            cxm[b, ch(c), :] = x_prev
            d = (
                cap[b, ch(c), :]
                + PAD_CONDUCTANCE * pm[b, ch(c), :].astype(jnp.float32)
                + x_here
                + y_all
                + vg[b, ch(c), :]
                + x_prev
                + pltpu.roll(y_in, 1, 1)
                + lower
            )
            r = 1.0 / d
            cy[b, ch(c), :] = y_in
            dg[b, ch(c), :] = d
            rd[b, ch(c), :] = r
            field[X0, b, fch(c), :] = ob[1, b, ch(c), :] * r
        send_planes(X0, c)
        send_edges(X0, i)

    def neighbours(f, b, c):
        v = field[f, b, fch(c), :]
        y = cy[b, ch(c), :]
        lo = halo[f, 0, ch(c), :] if b == 0 else field[f, 0, fch(c), :]
        hi = field[f, 1, fch(c), :] if b == 0 else halo[f, 1, ch(c), :]
        g_lo = below[ch(c), :] if b == 0 else vg[0, ch(c), :]
        total = (
            cx[b, fch(c), :] * row_after(v, field[f, b, fch(c + 1), :])
            + cxm[b, ch(c), :] * row_before(v, field[f, b, fch(c - 1), :])
            + vg[b, ch(c), :] * hi
            + g_lo * lo
            + y * pltpu.roll(v, cols - 1, 1)
            + pltpu.roll(y * v, 1, 1)
        )
        return v, total

    @pl.loop(0, n_ch)
    def _(i):
        c = order(i)
        take_edges(X0, i)
        take_planes(X0, c)
        for b in range(2):
            _, n = neighbours(X0, b, c)
            field[Z0, b, fch(c), :] = rd[b, ch(c), :] * n
        send_planes(Z0, c)
        send_edges(Z0, i)

    def second(fz, fu, plane_ways, edge_ways):
        @pl.loop(0, n_ch)
        def _(i):
            c = order(i)
            take_edges(fz, i)
            take_planes(fz, c)
            for b in range(2):
                z, n = neighbours(fz, b, c)
                dz = dg[b, ch(c), :] * z
                w = dz - n
                u = z - rd[b, ch(c), :] * n
                field[fu, b, fch(c), :] = u
                acc[0] += lane_sum(dz * z)
                acc[1] += lane_sum(w * z)
                acc[2] += lane_sum(w * u)
            plane_ways(c)
            send_edges(fu, i, edge_ways)

    def forward(f, b, c, with_hi):
        v = field[f, b, fch(c), :]
        s = cx[b, fch(c), :] * row_after(v, field[f, b, fch(c + 1), :]) + cy[b, ch(c), :] * pltpu.roll(v, cols - 1, 1)
        if b == 0:
            s = s + vg[0, ch(c), :] * field[f, 1, fch(c), :]
        elif with_hi:
            s = s + vg[1, ch(c), :] * halo[f, 1, ch(c), :]
        return v, s

    def all_sum(k):
        value = jnp.concatenate([jnp.sum(acc[q], axis=0, keepdims=True) for q in range(4)] * 2, axis=0)
        slot = 0
        for stage in range(3):
            ars[k, stage] = value
            copies = []
            for b, t in peers(stage):
                copies.append(
                    pltpu.make_async_remote_copy(
                        src_ref=ars.at[k, stage],
                        dst_ref=arr.at[k, slot],
                        send_sem=ars_sem.at[k, slot],
                        recv_sem=arr_sem.at[k, slot],
                        device_id=dev(b, t),
                        device_id_type=MESH,
                    )
                )
                slot += 1
            for copy in copies:
                copy.start()
            yield
            for copy in copies:
                copy.wait_recv()
            for n in range(slot - len(copies), slot):
                value = value + arr[k, n]
            for copy in copies:
                copy.wait_send()
        totals = jnp.sum(value, axis=1, keepdims=True)
        return totals[0:1], totals[1:2], totals[2:3], totals[3:4]

    def run(gen):
        while True:
            try:
                next(gen)
            except StopIteration as end:
                return end.value

    def weights(sums):
        rz, zw, uw, edges = sums
        uau = uw - 2.0 * edges
        step0 = rz / zw
        rz_next = step0 * step0 * uw - rz
        ratio = rz_next / rz
        curve = zw - 2.0 * step0 * uw + step0 * step0 * uau - ratio * ratio * zw
        step1 = rz_next / curve
        return step0 + step1 * (1.0 + ratio), -step1 * step0

    second(Z0, U0, lambda c: send_planes(U0, c), (0, 1))

    @pl.loop(0, n_ch)
    def _(i):
        c = order(i)
        take_edges(U0, i, (1,))
        take_planes(U0, c, (1,))
        for b in range(2):
            v, s = forward(U0, b, c, True)
            acc[3] += lane_sum(v * s)

    gen = all_sum(0)
    next(gen)

    @pl.loop(0, n_ch)
    def _(i):
        c = order(i)
        take_edges(U0, i, (0,))
        take_planes(U0, c, (0,))
        for b in range(2):
            _, n = neighbours(U0, b, c)
            qq[b, ch(c), :] = n

    ld[7].wait()
    w0, w1 = weights(run(gen))
    acc[...] = jnp.zeros_like(acc)

    @pl.loop(0, n_ch)
    def _(i):
        c = order(i)
        for b in range(2):
            x = field[X0, b, fch(c), :]
            z = field[Z0, b, fch(c), :]
            u = field[U0, b, fch(c), :]
            a = x + w0 * z + w1 * u
            adj[1, b, ch(c), :] = a
            inner = ob[0, b, ch(c), :] + cap[b, ch(c), :] * a + w1 * qq[b, ch(c), :]
            field[Z1, b, fch(c), :] = rd[b, ch(c), :] * inner - x + z - (w0 + w1) * u
        send_planes(Z1, c)
        send_edges(Z1, i)

    out1 = pltpu.make_async_copy(adj.at[1], out_hbm.at[1], out_sem.at[1])
    out1.start()

    half = n_ch // 2

    def half_planes(c):
        @pl.when(jnp.logical_and(c < half, has_dn))
        def _():
            plane_copy(U1, 1, c).start()

        @pl.when(jnp.logical_and(c >= half, has_up))
        def _():
            plane_copy(U1, 0, c).start()

    second(Z1, U1, half_planes, (1,))

    @pl.loop(0, n_ch)
    def _(i):
        c = order(i)
        take_edges(U1, i, (1,))
        for b in range(2):
            v, s = forward(U1, b, c, False)
            acc[3] += lane_sum(v * s)

        @pl.when(c < half)
        def _():
            take_planes(U1, c, (1,))

            @pl.when(has_up)
            def _():
                acc[3] += lane_sum(field[U1, 1, fch(c), :] * vg[1, ch(c), :] * halo[U1, 1, ch(c), :])

        @pl.when(c >= half)
        def _():
            take_planes(U1, c, (0,))

            @pl.when(has_dn)
            def _():
                acc[3] += lane_sum(field[U1, 0, fch(c), :] * below[ch(c), :] * halo[U1, 0, ch(c), :])

    w0, w1 = weights(run(all_sum(1)))

    @pl.loop(0, n_ch)
    def _(c):
        for b in range(2):
            adj[0, b, ch(c), :] = (
                adj[1, b, ch(c), :] + w0 * field[Z1, b, fch(c), :] + w1 * field[U1, b, fch(c), :]
            )

    out0 = pltpu.make_async_copy(adj.at[0], out_hbm.at[0], out_sem.at[0])
    out0.start()

    @pl.loop(0, n_ch)
    def _(c):
        @pl.when(has_up)
        def _():
            via_copy(c).wait_send()

        for f in range(5):
            for way in range(2):
                sent = has_dn if way else has_up
                if f == U1:
                    sent = jnp.logical_and(sent, c < half if way else c >= half)

                @pl.when(sent)
                def _():
                    plane_copy(f, way, c).wait_send()

    @pl.when(has_next)
    def _():
        for f in (X0, Z0, U0, Z1, CX):
            edge_copy(f, 0).wait_send()

    @pl.when(has_prev)
    def _():
        for f in (X0, Z0, U0, Z1, U1):
            edge_copy(f, 1).wait_send()

    out1.wait()
    out0.wait()


def on_device(cond_x, cond_y, via_cond, via_mask, capacitance, pad_mask, observe):
    _, rows, cols = cond_x.shape
    n_ch = rows // CH
    slots = TX - 1 + TZ - 1 + TY * 4 - 1
    block = pltpu.VMEM((2, rows, cols), jnp.float32)
    ints = pltpu.VMEM((2, rows, cols), jnp.int32)
    dma = pltpu.SemaphoreType.DMA
    return pl.pallas_call(
        kernel,
        out_shape=jax.ShapeDtypeStruct((2, 2, rows, cols), jnp.float32),
        in_specs=[pl.BlockSpec(memory_space=pl.ANY)] * 7,
        out_specs=pl.BlockSpec(memory_space=pl.ANY),
        scratch_shapes=[
            pltpu.VMEM((2, TOP + rows, cols), jnp.float32),
            block, block, ints, block, ints,
            pltpu.VMEM((2, 2, rows, cols), jnp.float32),
            block,
            block, block, block, block,
            pltpu.VMEM((5, 2, TOP + rows + 8, cols), jnp.float32),
            pltpu.VMEM((5, 2, rows, cols), jnp.float32),
            pltpu.VMEM((rows, cols), jnp.float32),
            pltpu.VMEM((6, 2, 2, cols), jnp.float32),
            pltpu.VMEM((6, 2, 2, cols), jnp.float32),
            pltpu.VMEM((4, 8, 128), jnp.float32),
            pltpu.VMEM((2, 3, 8, 128), jnp.float32),
            pltpu.VMEM((2, slots, 8, 128), jnp.float32),
            pltpu.VMEM((2, 2, rows, cols), jnp.float32),
            dma((8,)), dma((2,)),
            dma((5, 2, n_ch)), dma((5, 2, n_ch)), dma((n_ch,)), dma((n_ch,)),
            dma((6, 2)), dma((6, 2)), dma((2, slots)), dma((2, slots)),
        ],
        compiler_params=pltpu.CompilerParams(
            collective_id=0, has_side_effects=True, vmem_limit_bytes=60 * 1024 * 1024
        ),
    )(cond_x, cond_y, via_cond, via_mask, capacitance, pad_mask, observe)


def solution(mesh):
    placed = P("band", "tile", None)
    return jax.shard_map(
        on_device,
        mesh=mesh,
        in_specs=(placed,) * 6 + (P(None, "band", "tile", None),),
        out_specs=P(None, "band", "tile", None),
        check_vma=False,
    )
```

```python
import functools

import jax
import jax.numpy as jnp
from jax import lax
from jax.experimental import pallas as pl
from jax.experimental.pallas import tpu as pltpu
from jax.sharding import PartitionSpec as P

MESH = pl.DeviceIdType.MESH
PAD_CONDUCTANCE = 4.0
NB = 8
TY, TZ, TX = 2, 4, 4
CH = 8
UPWARD = 2
TOP = 8
X0, Z0, U0, Z1, U1 = range(5)
CX, DPART, OBS1, RD, OBS0, CAP, QQ = range(5, 12)


def lane_sum(p):
    parts = [p[:, k : k + 128] for k in range(0, p.shape[1], 128)]
    while len(parts) > 1:
        parts = [a + b for a, b in zip(parts[::2], parts[1::2])]
    return parts[0]


def kernel(
    cx_hbm, cy_hbm, vc_hbm, vm_hbm, cap_hbm, pm_hbm, ob_hbm, out_hbm,
    cx, cy, vc, vm, cap, pm, ob, vg, cxm, dg, rd, qq, field, halo, below, es, er, acc, ars, arr, adj,
    in_sem, out_sem, ps, pr, gs, gr, ess, ers, ars_sem, arr_sem,
):
    bands = lax.axis_size("band")
    tiles = lax.axis_size("tile")
    band = lax.axis_index("band")
    tile = lax.axis_index("tile")
    rows, cols = cy.shape[1], cy.shape[2]
    n_ch = rows // CH
    has_dn, has_up = band > 0, band < bands - 1
    has_prev, has_next = tile > 0, tile < tiles - 1

    def loads():
        pairs = [
            (vc_hbm, vc), (vm_hbm, vm), (cx_hbm, cx.at[:, pl.ds(TOP, rows), :]), (cy_hbm, cy), (cap_hbm, cap), (pm_hbm, pm),
            (ob_hbm.at[1], ob.at[1]), (ob_hbm.at[0], ob.at[0]),
        ]
        return [pltpu.make_async_copy(s, d, in_sem.at[k]) for k, (s, d) in enumerate(pairs)]

    ld = loads()
    for copy in ld:
        copy.start()

    tx = lax.rem(tile, TX)
    tz = lax.rem(lax.div(tile, TX), TZ)
    ty = lax.div(tile, TX * TZ)

    def peers(stage):
        if stage == 0:
            plane = tz * TX + tx
            return [(band, tile - plane + lax.rem(plane + d, TZ * TX)) for d in range(1, TZ * TX)]
        both = ty * bands + band
        out = []
        for d in range(1, TY * bands):
            other = lax.rem(both + d, TY * bands)
            out.append((lax.rem(other, bands), tile + (lax.div(other, bands) - ty) * (TX * TZ)))
        return out

    def dev(b, t):
        return {"band": b, "tile": t}

    barrier = pltpu.get_barrier_semaphore()
    known = [p for stage in range(2) for p in peers(stage)]
    for there, t in ((has_next, tile + 1), (has_prev, tile - 1)):
        @pl.when(there)
        def _():
            pl.semaphore_signal(barrier, inc=1, device_id=dev(band, t), device_id_type=MESH)
    for b, t in known:
        pl.semaphore_signal(barrier, inc=1, device_id=dev(b, t), device_id_type=MESH)

    zero_row = jnp.zeros((1, cols), jnp.float32)
    for f in range(5):
        for b in range(2):
            field[f, b, TOP - 1 : TOP, :] = zero_row
            field[f, b, TOP + rows : TOP + rows + 1, :] = zero_row

    @pl.when(jnp.logical_not(has_dn))
    def _():
        below[...] = jnp.zeros_like(below)

        @pl.loop(0, 5)
        def _(f):
            halo[f, 0] = jnp.zeros((rows, cols), jnp.float32)

    @pl.when(jnp.logical_not(has_up))
    def _():
        @pl.loop(0, 5)
        def _(f):
            halo[f, 1] = jnp.zeros((rows, cols), jnp.float32)

    acc[...] = jnp.zeros_like(acc)

    def ch(c):
        return pl.ds(pl.multiple_of(c * CH, CH), CH)

    def fch(c):
        return pl.ds(pl.multiple_of(TOP + c * CH, CH), CH)

    lane = lax.broadcasted_iota(jnp.int32, (CH, cols), 1)
    sub = lax.broadcasted_iota(jnp.int32, (CH, cols), 0)

    def row_after(here, after):
        return pltpu.roll(jnp.where(sub == 0, after, here), CH - 1, 0)

    def row_before(here, before):
        return pltpu.roll(jnp.where(sub == CH - 1, before, here), 1, 0)

    def plane_copy(f, way, c):
        return pltpu.make_async_remote_copy(
            src_ref=field.at[f, 1 - way, fch(c), :],
            dst_ref=halo.at[f, way, ch(c), :],
            send_sem=ps.at[f, way, c],
            recv_sem=pr.at[f, way, c],
            device_id=dev(band + 1 - 2 * way, tile),
            device_id_type=MESH,
        )

    def via_copy(c):
        return pltpu.make_async_remote_copy(
            src_ref=vg.at[1, ch(c), :],
            dst_ref=below.at[ch(c), :],
            send_sem=gs.at[c],
            recv_sem=gr.at[c],
            device_id=dev(band + 1, tile),
            device_id_type=MESH,
        )

    def edge_copy(f, way):
        return pltpu.make_async_remote_copy(
            src_ref=es.at[f, way],
            dst_ref=er.at[f, way],
            send_sem=ess.at[f, way],
            recv_sem=ers.at[f, way],
            device_id=dev(band, tile + 1 - 2 * way),
            device_id_type=MESH,
        )

    def send_edges(f, i, ways=(0, 1)):
        if 1 in ways:
            @pl.when(jnp.logical_and(i == 0, has_prev))
            def _():
                for b in range(2):
                    es[f, 1, b : b + 1, :] = field[f, b, TOP : TOP + 1, :]
                edge_copy(f, 1).start()
        if 0 in ways:
            @pl.when(jnp.logical_and(i == 1, has_next))
            def _():
                for b in range(2):
                    es[f, 0, b : b + 1, :] = field[f, b, TOP + rows - 1 : TOP + rows, :]
                edge_copy(f, 0).start()

    def take_edges(f, i, ways=(0, 1)):
        if 0 in ways:
            @pl.when(jnp.logical_and(i == 0, has_prev))
            def _():
                edge_copy(f, 0).wait_recv()
                for b in range(2):
                    field[f, b, TOP - 1 : TOP, :] = er[f, 0, b : b + 1, :]
        if 1 in ways and f == X0:
            @pl.when(jnp.logical_and(i == 1, has_next))
            def _():
                edge_copy(DPART, 1).wait_recv()
                edge_copy(OBS1, 1).wait_recv()
                for b in range(2):
                    r = 1.0 / (er[DPART, 1, b : b + 1, :] + cx[b, TOP + rows - 1 : TOP + rows, :])
                    er[RD, 1, b : b + 1, :] = r
                    field[X0, b, TOP + rows : TOP + rows + 1, :] = er[OBS1, 1, b : b + 1, :] * r
        elif 1 in ways:
            @pl.when(jnp.logical_and(i == 1, has_next))
            def _():
                edge_copy(f, 1).wait_recv()
                for b in range(2):
                    field[f, b, TOP + rows : TOP + rows + 1, :] = er[f, 1, b : b + 1, :]

    def send_planes(f, c, ways=(0, 1)):
        for way in ways:
            @pl.when(has_dn if way else has_up)
            def _():
                plane_copy(f, way, c).start()

    def take_planes(f, c, ways=(0, 1)):
        for way in ways:
            @pl.when(has_up if way else has_dn)
            def _():
                plane_copy(f, way, c).wait_recv()

    def order(i):
        return lax.rem(i * (n_ch - 1), n_ch)

    ld[0].wait()
    ld[1].wait()
    pl.semaphore_wait(barrier, len(known) + has_next.astype(jnp.int32) + has_prev.astype(jnp.int32))

    ld[2].wait()

    @pl.when(has_next)
    def _():
        for b in range(2):
            es[CX, 0, b : b + 1, :] = cx[b, TOP + rows - 1 : TOP + rows, :]
        edge_copy(CX, 0).start()

    @pl.loop(0, n_ch)
    def _(i):
        c = order(i)
        for b in range(2):
            keep = (band * 2 + b < NB - 1).astype(jnp.float32)
            vg[b, ch(c), :] = vc[b, ch(c), :] * vm[b, ch(c), :].astype(jnp.float32) * keep

        @pl.when(has_up)
        def _():
            via_copy(c).start()

    for b in range(2):
        cx[b, TOP - 1 : TOP, :] = zero_row
    for copy in ld[3:7]:
        copy.wait()

    def first_rows():
        for b in range(2):
            y_all = cy[b, 0:1, :]
            y_in = jnp.where(lane[0:1] == cols - 1, 0.0, y_all)
            es[DPART, 1, b : b + 1, :] = (
                cap[b, 0:1, :]
                + PAD_CONDUCTANCE * pm[b, 0:1, :].astype(jnp.float32)
                + cx[b, TOP : TOP + 1, :]
                + y_all
                + vg[b, 0:1, :]
                + pltpu.roll(y_in, 1, 1)
                + (below[0:1, :] if b == 0 else vg[0, 0:1, :])
            )
            es[OBS1, 1, b : b + 1, :] = ob[1, b, 0:1, :]
        edge_copy(DPART, 1).start()
        edge_copy(OBS1, 1).start()

    def take_row_before():
        edge_copy(CX, 0).wait_recv()
        for b in range(2):
            cx[b, TOP - 1 : TOP, :] = er[CX, 0, b : b + 1, :]

    def start_chunk(c):
        @pl.when(has_dn)
        def _():
            via_copy(c).wait_recv()

        if isinstance(c, int) and c == 0:
            @pl.when(has_prev)
            def _():
                first_rows()
                take_row_before()

        for b in range(2):
            y_all = cy[b, ch(c), :]
            y_in = jnp.where(lane == cols - 1, 0.0, y_all)
            lower = below[ch(c), :] if b == 0 else vg[0, ch(c), :]
            x_here = cx[b, fch(c), :]
            x_prev = row_before(x_here, cx[b, fch(c - 1), :])
            cxm[b, ch(c), :] = x_prev
            d = (
                cap[b, ch(c), :]
                + PAD_CONDUCTANCE * pm[b, ch(c), :].astype(jnp.float32)
                + x_here
                + y_all
                + vg[b, ch(c), :]
                + x_prev
                + pltpu.roll(y_in, 1, 1)
                + lower
            )
            r = 1.0 / d
            cy[b, ch(c), :] = y_in
            dg[b, ch(c), :] = d
            rd[b, ch(c), :] = r
            field[X0, b, fch(c), :] = ob[1, b, ch(c), :] * r
        send_planes(X0, c)

    start_chunk(n_ch - 1)

    @pl.when(has_next)
    def _():
        for b in range(2):
            es[X0, 0, b : b + 1, :] = field[X0, b, TOP + rows - 1 : TOP + rows, :]
        edge_copy(X0, 0).start()

    start_chunk(0)

    @pl.loop(2, n_ch)
    def _(i):
        start_chunk(n_ch - i)

    ld[7].wait()

    @pl.when(has_next)
    def _():
        for b in range(2):
            es[RD, 0, b : b + 1, :] = rd[b, rows - 1 : rows, :]
            es[OBS0, 0, b : b + 1, :] = ob[0, b, rows - 1 : rows, :]
            es[CAP, 0, b : b + 1, :] = cap[b, rows - 1 : rows, :]
        for f in (RD, OBS0, CAP):
            edge_copy(f, 0).start()

    @pl.when(has_prev)
    def _():
        for b in range(2):
            es[OBS0, 1, b : b + 1, :] = ob[0, b, 0:1, :]
            es[CAP, 1, b : b + 1, :] = cap[b, 0:1, :]
        for f in (OBS0, CAP):
            edge_copy(f, 1).start()

    def neighbours(f, b, c):
        v = field[f, b, fch(c), :]
        y = cy[b, ch(c), :]
        lo = halo[f, 0, ch(c), :] if b == 0 else field[f, 0, fch(c), :]
        hi = field[f, 1, fch(c), :] if b == 0 else halo[f, 1, ch(c), :]
        g_lo = below[ch(c), :] if b == 0 else vg[0, ch(c), :]
        total = (
            cx[b, fch(c), :] * row_after(v, field[f, b, fch(c + 1), :])
            + cxm[b, ch(c), :] * row_before(v, field[f, b, fch(c - 1), :])
            + vg[b, ch(c), :] * hi
            + g_lo * lo
            + y * pltpu.roll(v, cols - 1, 1)
            + pltpu.roll(y * v, 1, 1)
        )
        return v, total

    @pl.loop(0, n_ch)
    def _(i):
        c = order(i)
        take_edges(X0, i)
        take_planes(X0, c)
        for b in range(2):
            _, n = neighbours(X0, b, c)
            field[Z0, b, fch(c), :] = rd[b, ch(c), :] * n
        send_planes(Z0, c)
        send_edges(Z0, i)

    def second(fz, fu, plane_ways, edge_ways):
        @pl.loop(0, n_ch)
        def _(i):
            c = order(i)
            if fz != Z1:
                take_edges(fz, i)
            take_planes(fz, c)
            for b in range(2):
                z, n = neighbours(fz, b, c)
                dz = dg[b, ch(c), :] * z
                w = dz - n
                u = z - rd[b, ch(c), :] * n
                field[fu, b, fch(c), :] = u
                acc[0] += lane_sum(dz * z)
                acc[1] += lane_sum(w * z)
                acc[2] += lane_sum(w * u)
            plane_ways(c)
            send_edges(fu, i, edge_ways)

    def forward(f, b, c):
        v = field[f, b, fch(c), :]
        s = cx[b, fch(c), :] * row_after(v, field[f, b, fch(c + 1), :]) + cy[b, ch(c), :] * pltpu.roll(v, cols - 1, 1)
        if b == 0:
            s = s + vg[0, ch(c), :] * field[f, 1, fch(c), :]
        return v, s

    def between(f, c, low, high):
        @pl.when(jnp.logical_and(low, has_up))
        def _():
            plane_copy(f, 1, c).wait_recv()
            acc[3] += lane_sum(field[f, 1, fch(c), :] * vg[1, ch(c), :] * halo[f, 1, ch(c), :])

        @pl.when(jnp.logical_and(high, has_dn))
        def _():
            plane_copy(f, 0, c).wait_recv()
            acc[3] += lane_sum(field[f, 0, fch(c), :] * below[ch(c), :] * halo[f, 0, ch(c), :])

    def all_sum(k):
        value = jnp.concatenate([jnp.sum(acc[q], axis=0, keepdims=True) for q in range(4)] * 2, axis=0)
        slot = 0
        for stage in range(2):
            ars[k, stage] = value
            copies = []
            for b, t in peers(stage):
                copies.append(
                    pltpu.make_async_remote_copy(
                        src_ref=ars.at[k, stage],
                        dst_ref=arr.at[k, slot],
                        send_sem=ars_sem.at[k, slot],
                        recv_sem=arr_sem.at[k, slot],
                        device_id=dev(b, t),
                        device_id_type=MESH,
                    )
                )
                slot += 1
            for copy in copies:
                copy.start()
            yield
            for copy in copies:
                copy.wait_recv()
            for n in range(slot - len(copies), slot):
                value = value + arr[k, n]
            for copy in copies:
                copy.wait_send()
        totals = jnp.sum(value, axis=1, keepdims=True)
        return totals[0:1], totals[1:2], totals[2:3], totals[3:4]

    def run(gen):
        while True:
            try:
                next(gen)
            except StopIteration as end:
                return end.value

    def weights(sums):
        rz, zw, uw, edges = sums
        uau = uw - 2.0 * edges
        step0 = rz / zw
        rz_next = step0 * step0 * uw - rz
        ratio = rz_next / rz
        curve = zw - 2.0 * step0 * uw + step0 * step0 * uau - ratio * ratio * zw
        step1 = rz_next / curve
        return step0 + step1 * (1.0 + ratio), -step1 * step0

    def urgent(c):
        @pl.when(jnp.logical_and(is_low(c), has_dn))
        def _():
            plane_copy(U0, 1, c).start()

        @pl.when(jnp.logical_and(is_high(c), has_up))
        def _():
            plane_copy(U0, 0, c).start()

    def is_high(c):
        return jnp.logical_and(c >= 1, c <= UPWARD)

    def is_low(c):
        return jnp.logical_or(c == 0, c > UPWARD)

    second(Z0, U0, urgent, (0, 1))

    @pl.loop(0, n_ch)
    def _(i):
        c = order(i)

        @pl.when(jnp.logical_and(is_high(c), has_dn))
        def _():
            plane_copy(U0, 1, c).start()

        @pl.when(jnp.logical_and(is_low(c), has_up))
        def _():
            plane_copy(U0, 0, c).start()

    @pl.loop(0, n_ch)
    def _(i):
        c = order(i)
        take_edges(U0, i, (1,))
        for b in range(2):
            v, s = forward(U0, b, c)
            acc[3] += lane_sum(v * s)
        between(U0, c, is_low(c), is_high(c))

    gen = all_sum(0)
    next(gen)

    @pl.loop(0, n_ch)
    def _(i):
        c = order(i)
        take_edges(U0, i, (0,))

        @pl.when(jnp.logical_and(is_high(c), has_up))
        def _():
            plane_copy(U0, 1, c).wait_recv()

        @pl.when(jnp.logical_and(is_low(c), has_dn))
        def _():
            plane_copy(U0, 0, c).wait_recv()

        for b in range(2):
            _, n = neighbours(U0, b, c)
            qq[b, ch(c), :] = n

        @pl.when(jnp.logical_and(i == 0, has_prev))
        def _():
            for b in range(2):
                es[QQ, 1, b : b + 1, :] = qq[b, 0:1, :]
            edge_copy(QQ, 1).start()

        @pl.when(jnp.logical_and(i == 1, has_next))
        def _():
            for b in range(2):
                es[QQ, 0, b : b + 1, :] = qq[b, rows - 1 : rows, :]
            edge_copy(QQ, 0).start()

    w0, w1 = weights(run(gen))
    acc[...] = jnp.zeros_like(acc)

    @pl.loop(0, n_ch)
    def _(i):
        c = order(i)
        for b in range(2):
            x = field[X0, b, fch(c), :]
            z = field[Z0, b, fch(c), :]
            u = field[U0, b, fch(c), :]
            a = x + w0 * z + w1 * u
            adj[1, b, ch(c), :] = a
            inner = ob[0, b, ch(c), :] + cap[b, ch(c), :] * a + w1 * qq[b, ch(c), :]
            field[Z1, b, fch(c), :] = rd[b, ch(c), :] * inner - x + z - (w0 + w1) * u
        send_planes(Z1, c)

    def beside(way, at):
        edge_copy(QQ, way).wait_recv()
        for f in (RD, OBS0, CAP) if way == 0 else (OBS0, CAP):
            edge_copy(f, way).wait_recv()
        for b in range(2):
            x = field[X0, b, at : at + 1, :]
            z = field[Z0, b, at : at + 1, :]
            u = field[U0, b, at : at + 1, :]
            row = [er[f, way, b : b + 1, :] for f in (RD, OBS0, CAP, QQ)]
            inner = row[1] + row[2] * (x + w0 * z + w1 * u) + w1 * row[3]
            field[Z1, b, at : at + 1, :] = row[0] * inner - x + z - (w0 + w1) * u

    @pl.when(has_prev)
    def _():
        beside(0, TOP - 1)

    @pl.when(has_next)
    def _():
        beside(1, TOP + rows)

    out1 = pltpu.make_async_copy(adj.at[1], out_hbm.at[1], out_sem.at[1])
    out1.start()

    half = n_ch // 2

    def half_planes(c):
        @pl.when(jnp.logical_and(c < half, has_dn))
        def _():
            plane_copy(U1, 1, c).start()

        @pl.when(jnp.logical_and(c >= half, has_up))
        def _():
            plane_copy(U1, 0, c).start()

    second(Z1, U1, half_planes, (1,))

    @pl.loop(0, n_ch)
    def _(i):
        c = order(i)
        take_edges(U1, i, (1,))
        for b in range(2):
            v, s = forward(U1, b, c)
            acc[3] += lane_sum(v * s)
        between(U1, c, c < half, c >= half)

    w0, w1 = weights(run(all_sum(1)))

    @pl.loop(0, n_ch)
    def _(c):
        for b in range(2):
            adj[0, b, ch(c), :] = (
                adj[1, b, ch(c), :] + w0 * field[Z1, b, fch(c), :] + w1 * field[U1, b, fch(c), :]
            )

    out0 = pltpu.make_async_copy(adj.at[0], out_hbm.at[0], out_sem.at[0])
    out0.start()

    @pl.loop(0, n_ch)
    def _(c):
        @pl.when(has_up)
        def _():
            via_copy(c).wait_send()

        for f in range(5):
            for way in range(2):
                sent = has_dn if way else has_up
                if f == U1:
                    sent = jnp.logical_and(sent, c < half if way else c >= half)

                @pl.when(sent)
                def _():
                    plane_copy(f, way, c).wait_send()

    @pl.when(has_next)
    def _():
        for f in (X0, Z0, U0, CX, RD, OBS0, CAP, QQ):
            edge_copy(f, 0).wait_send()

    @pl.when(has_prev)
    def _():
        for f in (Z0, U0, U1, DPART, OBS1, OBS0, CAP, QQ):
            edge_copy(f, 1).wait_send()

    out1.wait()
    out0.wait()


def on_device(cond_x, cond_y, via_cond, via_mask, capacitance, pad_mask, observe):
    _, rows, cols = cond_x.shape
    n_ch = rows // CH
    slots = TX * TZ - 1 + TY * 4 - 1
    block = pltpu.VMEM((2, rows, cols), jnp.float32)
    ints = pltpu.VMEM((2, rows, cols), jnp.int32)
    dma = pltpu.SemaphoreType.DMA
    return pl.pallas_call(
        kernel,
        out_shape=jax.ShapeDtypeStruct((2, 2, rows, cols), jnp.float32),
        in_specs=[pl.BlockSpec(memory_space=pl.ANY)] * 7,
        out_specs=pl.BlockSpec(memory_space=pl.ANY),
        scratch_shapes=[
            pltpu.VMEM((2, TOP + rows, cols), jnp.float32),
            block, block, ints, block, ints,
            pltpu.VMEM((2, 2, rows, cols), jnp.float32),
            block,
            block, block, block, block,
            pltpu.VMEM((5, 2, TOP + rows + 8, cols), jnp.float32),
            pltpu.VMEM((5, 2, rows, cols), jnp.float32),
            pltpu.VMEM((rows, cols), jnp.float32),
            pltpu.VMEM((12, 2, 2, cols), jnp.float32),
            pltpu.VMEM((12, 2, 2, cols), jnp.float32),
            pltpu.VMEM((4, 8, 128), jnp.float32),
            pltpu.VMEM((2, 2, 8, 128), jnp.float32),
            pltpu.VMEM((2, slots, 8, 128), jnp.float32),
            pltpu.VMEM((2, 2, rows, cols), jnp.float32),
            dma((8,)), dma((2,)),
            dma((5, 2, n_ch)), dma((5, 2, n_ch)), dma((n_ch,)), dma((n_ch,)),
            dma((12, 2)), dma((12, 2)), dma((2, slots)), dma((2, slots)),
        ],
        compiler_params=pltpu.CompilerParams(
            collective_id=0, has_side_effects=True, vmem_limit_bytes=60 * 1024 * 1024
        ),
    )(cond_x, cond_y, via_cond, via_mask, capacitance, pad_mask, observe)


def solution(mesh):
    placed = P("band", "tile", None)
    return jax.shard_map(
        on_device,
        mesh=mesh,
        in_specs=(placed,) * 6 + (P(None, "band", "tile", None),),
        out_specs=P(None, "band", "tile", None),
        check_vma=False,
    )
```

```python
import functools

import jax
import jax.numpy as jnp
from jax import lax
from jax.experimental import pallas as pl
from jax.experimental.pallas import tpu as pltpu
from jax.sharding import PartitionSpec as P

MESH = pl.DeviceIdType.MESH
PAD_CONDUCTANCE = 4.0
NB = 8
TY, TZ, TX = 2, 4, 4
CH = 8
UPWARD = 2
TOP = 8
X0, Z0, U0, Z1, U1 = range(5)
CX, DPART, OBS1, RD, OBS0, CAP, QQ = range(5, 12)


def lane_sum(p):
    parts = [p[:, k : k + 128] for k in range(0, p.shape[1], 128)]
    while len(parts) > 1:
        parts = [a + b for a, b in zip(parts[::2], parts[1::2])]
    return parts[0]


def kernel(
    cx_hbm, cy_hbm, vc_hbm, vm_hbm, cap_hbm, pm_hbm, ob_hbm, adj0, adj1,
    cx, cy, vc, vm, cap, pm, ob, vg, cxm, dg, rd, qq, field, halo, below, es, er, acc, ars, arr,
    in_sem, ps, pr, gs, gr, ess, ers, ars_sem, arr_sem,
):
    bands = lax.axis_size("band")
    tiles = lax.axis_size("tile")
    band = lax.axis_index("band")
    tile = lax.axis_index("tile")
    rows, cols = cy.shape[1], cy.shape[2]
    n_ch = rows // CH
    has_dn, has_up = band > 0, band < bands - 1
    has_prev, has_next = tile > 0, tile < tiles - 1

    def loads():
        pairs = [
            (vc_hbm, vc), (vm_hbm, vm), (cx_hbm, cx.at[:, pl.ds(TOP, rows), :]), (cy_hbm, cy), (cap_hbm, cap), (pm_hbm, pm),
            (ob_hbm.at[1], ob.at[1]), (ob_hbm.at[0], ob.at[0]),
        ]
        return [pltpu.make_async_copy(s, d, in_sem.at[k]) for k, (s, d) in enumerate(pairs)]

    ld = loads()
    for copy in ld:
        copy.start()

    tx = lax.rem(tile, TX)
    tz = lax.rem(lax.div(tile, TX), TZ)
    ty = lax.div(tile, TX * TZ)

    def peers(stage):
        if stage == 0:
            plane = tz * TX + tx
            return [(band, tile - plane + lax.rem(plane + d, TZ * TX)) for d in range(1, TZ * TX)]
        both = ty * bands + band
        out = []
        for d in range(1, TY * bands):
            other = lax.rem(both + d, TY * bands)
            out.append((lax.rem(other, bands), tile + (lax.div(other, bands) - ty) * (TX * TZ)))
        return out

    def dev(b, t):
        return {"band": b, "tile": t}

    barrier = pltpu.get_barrier_semaphore()
    known = [p for stage in range(2) for p in peers(stage)]
    for there, t in ((has_next, tile + 1), (has_prev, tile - 1)):
        @pl.when(there)
        def _():
            pl.semaphore_signal(barrier, inc=1, device_id=dev(band, t), device_id_type=MESH)
    for b, t in known:
        pl.semaphore_signal(barrier, inc=1, device_id=dev(b, t), device_id_type=MESH)

    zero_row = jnp.zeros((1, cols), jnp.float32)
    for f in range(5):
        for b in range(2):
            field[f, b, TOP - 1 : TOP, :] = zero_row
            field[f, b, TOP + rows : TOP + rows + 1, :] = zero_row

    @pl.when(jnp.logical_not(has_dn))
    def _():
        below[...] = jnp.zeros_like(below)

        @pl.loop(0, 5)
        def _(f):
            halo[f, 0] = jnp.zeros((rows, cols), jnp.float32)

    @pl.when(jnp.logical_not(has_up))
    def _():
        @pl.loop(0, 5)
        def _(f):
            halo[f, 1] = jnp.zeros((rows, cols), jnp.float32)

    acc[...] = jnp.zeros_like(acc)

    def ch(c):
        return pl.ds(pl.multiple_of(c * CH, CH), CH)

    def fch(c):
        return pl.ds(pl.multiple_of(TOP + c * CH, CH), CH)

    lane = lax.broadcasted_iota(jnp.int32, (CH, cols), 1)
    sub = lax.broadcasted_iota(jnp.int32, (CH, cols), 0)

    def row_after(here, after):
        return pltpu.roll(jnp.where(sub == 0, after, here), CH - 1, 0)

    def row_before(here, before):
        return pltpu.roll(jnp.where(sub == CH - 1, before, here), 1, 0)

    def plane_copy(f, way, c):
        return pltpu.make_async_remote_copy(
            src_ref=field.at[f, 1 - way, fch(c), :],
            dst_ref=halo.at[f, way, ch(c), :],
            send_sem=ps.at[f, way, c],
            recv_sem=pr.at[f, way, c],
            device_id=dev(band + 1 - 2 * way, tile),
            device_id_type=MESH,
        )

    def via_copy(c):
        return pltpu.make_async_remote_copy(
            src_ref=vg.at[1, ch(c), :],
            dst_ref=below.at[ch(c), :],
            send_sem=gs.at[c],
            recv_sem=gr.at[c],
            device_id=dev(band + 1, tile),
            device_id_type=MESH,
        )

    def edge_copy(f, way):
        return pltpu.make_async_remote_copy(
            src_ref=es.at[f, way],
            dst_ref=er.at[f, way],
            send_sem=ess.at[f, way],
            recv_sem=ers.at[f, way],
            device_id=dev(band, tile + 1 - 2 * way),
            device_id_type=MESH,
        )

    def send_edges(f, i, ways=(0, 1)):
        if 1 in ways:
            @pl.when(jnp.logical_and(i == 0, has_prev))
            def _():
                for b in range(2):
                    es[f, 1, b : b + 1, :] = field[f, b, TOP : TOP + 1, :]
                edge_copy(f, 1).start()
        if 0 in ways:
            @pl.when(jnp.logical_and(i == 1, has_next))
            def _():
                for b in range(2):
                    es[f, 0, b : b + 1, :] = field[f, b, TOP + rows - 1 : TOP + rows, :]
                edge_copy(f, 0).start()

    def take_edges(f, i, ways=(0, 1)):
        if 0 in ways:
            @pl.when(jnp.logical_and(i == 0, has_prev))
            def _():
                edge_copy(f, 0).wait_recv()
                for b in range(2):
                    field[f, b, TOP - 1 : TOP, :] = er[f, 0, b : b + 1, :]
        if 1 in ways and f == X0:
            @pl.when(jnp.logical_and(i == 1, has_next))
            def _():
                edge_copy(DPART, 1).wait_recv()
                edge_copy(OBS1, 1).wait_recv()
                for b in range(2):
                    r = 1.0 / (er[DPART, 1, b : b + 1, :] + cx[b, TOP + rows - 1 : TOP + rows, :])
                    er[RD, 1, b : b + 1, :] = r
                    field[X0, b, TOP + rows : TOP + rows + 1, :] = er[OBS1, 1, b : b + 1, :] * r
        elif 1 in ways:
            @pl.when(jnp.logical_and(i == 1, has_next))
            def _():
                edge_copy(f, 1).wait_recv()
                for b in range(2):
                    field[f, b, TOP + rows : TOP + rows + 1, :] = er[f, 1, b : b + 1, :]

    def send_planes(f, c, ways=(0, 1)):
        for way in ways:
            @pl.when(has_dn if way else has_up)
            def _():
                plane_copy(f, way, c).start()

    def take_planes(f, c, ways=(0, 1)):
        for way in ways:
            @pl.when(has_up if way else has_dn)
            def _():
                plane_copy(f, way, c).wait_recv()

    def order(i):
        return lax.rem(i * (n_ch - 1), n_ch)

    ld[0].wait()
    ld[1].wait()
    pl.semaphore_wait(barrier, len(known) + has_next.astype(jnp.int32) + has_prev.astype(jnp.int32))

    ld[2].wait()

    @pl.when(has_next)
    def _():
        for b in range(2):
            es[CX, 0, b : b + 1, :] = cx[b, TOP + rows - 1 : TOP + rows, :]
        edge_copy(CX, 0).start()

    @pl.loop(0, n_ch)
    def _(i):
        c = order(i)
        for b in range(2):
            keep = (band * 2 + b < NB - 1).astype(jnp.float32)
            vg[b, ch(c), :] = vc[b, ch(c), :] * vm[b, ch(c), :].astype(jnp.float32) * keep

        @pl.when(has_up)
        def _():
            via_copy(c).start()

    for b in range(2):
        cx[b, TOP - 1 : TOP, :] = zero_row
    for copy in ld[3:7]:
        copy.wait()

    def first_rows():
        for b in range(2):
            y_all = cy[b, 0:1, :]
            y_in = jnp.where(lane[0:1] == cols - 1, 0.0, y_all)
            es[DPART, 1, b : b + 1, :] = (
                cap[b, 0:1, :]
                + PAD_CONDUCTANCE * pm[b, 0:1, :].astype(jnp.float32)
                + cx[b, TOP : TOP + 1, :]
                + y_all
                + vg[b, 0:1, :]
                + pltpu.roll(y_in, 1, 1)
                + (below[0:1, :] if b == 0 else vg[0, 0:1, :])
            )
            es[OBS1, 1, b : b + 1, :] = ob[1, b, 0:1, :]
        edge_copy(DPART, 1).start()
        edge_copy(OBS1, 1).start()

    def take_row_before():
        edge_copy(CX, 0).wait_recv()
        for b in range(2):
            cx[b, TOP - 1 : TOP, :] = er[CX, 0, b : b + 1, :]

    def start_chunk(c):
        @pl.when(has_dn)
        def _():
            via_copy(c).wait_recv()

        if isinstance(c, int) and c == 0:
            @pl.when(has_prev)
            def _():
                first_rows()
                take_row_before()

        for b in range(2):
            y_all = cy[b, ch(c), :]
            y_in = jnp.where(lane == cols - 1, 0.0, y_all)
            lower = below[ch(c), :] if b == 0 else vg[0, ch(c), :]
            x_here = cx[b, fch(c), :]
            x_prev = row_before(x_here, cx[b, fch(c - 1), :])
            cxm[b, ch(c), :] = x_prev
            d = (
                cap[b, ch(c), :]
                + PAD_CONDUCTANCE * pm[b, ch(c), :].astype(jnp.float32)
                + x_here
                + y_all
                + vg[b, ch(c), :]
                + x_prev
                + pltpu.roll(y_in, 1, 1)
                + lower
            )
            r = 1.0 / d
            cy[b, ch(c), :] = y_in
            dg[b, ch(c), :] = d
            rd[b, ch(c), :] = r
            field[X0, b, fch(c), :] = ob[1, b, ch(c), :] * r
        send_planes(X0, c)

    start_chunk(n_ch - 1)

    @pl.when(has_next)
    def _():
        for b in range(2):
            es[X0, 0, b : b + 1, :] = field[X0, b, TOP + rows - 1 : TOP + rows, :]
        edge_copy(X0, 0).start()

    start_chunk(0)

    @pl.loop(2, n_ch)
    def _(i):
        start_chunk(n_ch - i)

    ld[7].wait()

    @pl.when(has_next)
    def _():
        for b in range(2):
            es[RD, 0, b : b + 1, :] = rd[b, rows - 1 : rows, :]
            es[OBS0, 0, b : b + 1, :] = ob[0, b, rows - 1 : rows, :]
            es[CAP, 0, b : b + 1, :] = cap[b, rows - 1 : rows, :]
        for f in (RD, OBS0, CAP):
            edge_copy(f, 0).start()

    @pl.when(has_prev)
    def _():
        for b in range(2):
            es[OBS0, 1, b : b + 1, :] = ob[0, b, 0:1, :]
            es[CAP, 1, b : b + 1, :] = cap[b, 0:1, :]
        for f in (OBS0, CAP):
            edge_copy(f, 1).start()

    def neighbours(f, b, c):
        v = field[f, b, fch(c), :]
        y = cy[b, ch(c), :]
        lo = halo[f, 0, ch(c), :] if b == 0 else field[f, 0, fch(c), :]
        hi = field[f, 1, fch(c), :] if b == 0 else halo[f, 1, ch(c), :]
        g_lo = below[ch(c), :] if b == 0 else vg[0, ch(c), :]
        total = (
            cx[b, fch(c), :] * row_after(v, field[f, b, fch(c + 1), :])
            + cxm[b, ch(c), :] * row_before(v, field[f, b, fch(c - 1), :])
            + vg[b, ch(c), :] * hi
            + g_lo * lo
            + y * pltpu.roll(v, cols - 1, 1)
            + pltpu.roll(y * v, 1, 1)
        )
        return v, total

    @pl.loop(0, n_ch)
    def _(i):
        c = order(i)
        take_edges(X0, i)
        take_planes(X0, c)
        for b in range(2):
            _, n = neighbours(X0, b, c)
            field[Z0, b, fch(c), :] = rd[b, ch(c), :] * n
        send_planes(Z0, c)
        send_edges(Z0, i)

    def second(fz, fu, plane_ways, edge_ways):
        @pl.loop(0, n_ch)
        def _(i):
            c = order(i)
            if fz != Z1:
                take_edges(fz, i)
            take_planes(fz, c)
            for b in range(2):
                z, n = neighbours(fz, b, c)
                dz = dg[b, ch(c), :] * z
                w = dz - n
                u = z - rd[b, ch(c), :] * n
                field[fu, b, fch(c), :] = u
                acc[0] += lane_sum(dz * z)
                acc[1] += lane_sum(w * z)
                acc[2] += lane_sum(w * u)
            plane_ways(c)
            send_edges(fu, i, edge_ways)

    def forward(f, b, c):
        v = field[f, b, fch(c), :]
        s = cx[b, fch(c), :] * row_after(v, field[f, b, fch(c + 1), :]) + cy[b, ch(c), :] * pltpu.roll(v, cols - 1, 1)
        if b == 0:
            s = s + vg[0, ch(c), :] * field[f, 1, fch(c), :]
        return v, s

    def between(f, c, low, high):
        @pl.when(jnp.logical_and(low, has_up))
        def _():
            plane_copy(f, 1, c).wait_recv()
            acc[3] += lane_sum(field[f, 1, fch(c), :] * vg[1, ch(c), :] * halo[f, 1, ch(c), :])

        @pl.when(jnp.logical_and(high, has_dn))
        def _():
            plane_copy(f, 0, c).wait_recv()
            acc[3] += lane_sum(field[f, 0, fch(c), :] * below[ch(c), :] * halo[f, 0, ch(c), :])

    def all_sum(k):
        value = jnp.concatenate([jnp.sum(acc[q], axis=0, keepdims=True) for q in range(4)] * 2, axis=0)
        slot = 0
        for stage in range(2):
            ars[k, stage] = value
            copies = []
            for b, t in peers(stage):
                copies.append(
                    pltpu.make_async_remote_copy(
                        src_ref=ars.at[k, stage],
                        dst_ref=arr.at[k, slot],
                        send_sem=ars_sem.at[k, slot],
                        recv_sem=arr_sem.at[k, slot],
                        device_id=dev(b, t),
                        device_id_type=MESH,
                    )
                )
                slot += 1
            for copy in copies:
                copy.start()
            yield
            for copy in copies:
                copy.wait_recv()
            for n in range(slot - len(copies), slot):
                value = value + arr[k, n]
            for copy in copies:
                copy.wait_send()
        totals = jnp.sum(value, axis=1, keepdims=True)
        return totals[0:1], totals[1:2], totals[2:3], totals[3:4]

    def run(gen):
        while True:
            try:
                next(gen)
            except StopIteration as end:
                return end.value

    def weights(sums):
        rz, zw, uw, edges = sums
        uau = uw - 2.0 * edges
        step0 = rz / zw
        rz_next = step0 * step0 * uw - rz
        ratio = rz_next / rz
        curve = zw - 2.0 * step0 * uw + step0 * step0 * uau - ratio * ratio * zw
        step1 = rz_next / curve
        return step0 + step1 * (1.0 + ratio), -step1 * step0

    def urgent(c):
        @pl.when(jnp.logical_and(is_low(c), has_dn))
        def _():
            plane_copy(U0, 1, c).start()

        @pl.when(jnp.logical_and(is_high(c), has_up))
        def _():
            plane_copy(U0, 0, c).start()

    def is_high(c):
        return jnp.logical_and(c >= 1, c <= UPWARD)

    def is_low(c):
        return jnp.logical_or(c == 0, c > UPWARD)

    second(Z0, U0, urgent, (0, 1))

    @pl.loop(0, n_ch)
    def _(i):
        c = order(i)

        @pl.when(jnp.logical_and(is_high(c), has_dn))
        def _():
            plane_copy(U0, 1, c).start()

        @pl.when(jnp.logical_and(is_low(c), has_up))
        def _():
            plane_copy(U0, 0, c).start()

    @pl.loop(0, n_ch)
    def _(i):
        c = order(i)
        take_edges(U0, i, (1,))
        for b in range(2):
            v, s = forward(U0, b, c)
            acc[3] += lane_sum(v * s)
        between(U0, c, is_low(c), is_high(c))

    gen = all_sum(0)
    next(gen)

    @pl.loop(0, n_ch)
    def _(i):
        c = order(i)
        take_edges(U0, i, (0,))

        @pl.when(jnp.logical_and(is_high(c), has_up))
        def _():
            plane_copy(U0, 1, c).wait_recv()

        @pl.when(jnp.logical_and(is_low(c), has_dn))
        def _():
            plane_copy(U0, 0, c).wait_recv()

        for b in range(2):
            _, n = neighbours(U0, b, c)
            qq[b, ch(c), :] = n

        @pl.when(jnp.logical_and(i == 0, has_prev))
        def _():
            for b in range(2):
                es[QQ, 1, b : b + 1, :] = qq[b, 0:1, :]
            edge_copy(QQ, 1).start()

        @pl.when(jnp.logical_and(i == 1, has_next))
        def _():
            for b in range(2):
                es[QQ, 0, b : b + 1, :] = qq[b, rows - 1 : rows, :]
            edge_copy(QQ, 0).start()

    w0, w1 = weights(run(gen))
    acc[...] = jnp.zeros_like(acc)

    @pl.loop(0, n_ch)
    def _(i):
        c = order(i)
        for b in range(2):
            x = field[X0, b, fch(c), :]
            z = field[Z0, b, fch(c), :]
            u = field[U0, b, fch(c), :]
            a = x + w0 * z + w1 * u
            adj1[b, ch(c), :] = a
            inner = ob[0, b, ch(c), :] + cap[b, ch(c), :] * a + w1 * qq[b, ch(c), :]
            field[Z1, b, fch(c), :] = rd[b, ch(c), :] * inner - x + z - (w0 + w1) * u
        send_planes(Z1, c)

    def beside(way, at):
        edge_copy(QQ, way).wait_recv()
        for f in (RD, OBS0, CAP) if way == 0 else (OBS0, CAP):
            edge_copy(f, way).wait_recv()
        for b in range(2):
            x = field[X0, b, at : at + 1, :]
            z = field[Z0, b, at : at + 1, :]
            u = field[U0, b, at : at + 1, :]
            row = [er[f, way, b : b + 1, :] for f in (RD, OBS0, CAP, QQ)]
            inner = row[1] + row[2] * (x + w0 * z + w1 * u) + w1 * row[3]
            field[Z1, b, at : at + 1, :] = row[0] * inner - x + z - (w0 + w1) * u

    @pl.when(has_prev)
    def _():
        beside(0, TOP - 1)

    @pl.when(has_next)
    def _():
        beside(1, TOP + rows)

    half = n_ch // 2

    def half_planes(c):
        @pl.when(jnp.logical_and(c < half, has_dn))
        def _():
            plane_copy(U1, 1, c).start()

        @pl.when(jnp.logical_and(c >= half, has_up))
        def _():
            plane_copy(U1, 0, c).start()

    second(Z1, U1, half_planes, (1,))

    @pl.loop(0, n_ch)
    def _(i):
        c = order(i)
        take_edges(U1, i, (1,))
        for b in range(2):
            v, s = forward(U1, b, c)
            acc[3] += lane_sum(v * s)
        between(U1, c, c < half, c >= half)

    w0, w1 = weights(run(all_sum(1)))

    @pl.loop(0, n_ch)
    def _(c):
        for b in range(2):
            adj0[b, ch(c), :] = (
                adj1[b, ch(c), :] + w0 * field[Z1, b, fch(c), :] + w1 * field[U1, b, fch(c), :]
            )

    @pl.loop(0, n_ch)
    def _(c):
        @pl.when(has_up)
        def _():
            via_copy(c).wait_send()

        for f in range(5):
            for way in range(2):
                sent = has_dn if way else has_up
                if f == U1:
                    sent = jnp.logical_and(sent, c < half if way else c >= half)

                @pl.when(sent)
                def _():
                    plane_copy(f, way, c).wait_send()

    @pl.when(has_next)
    def _():
        for f in (X0, Z0, U0, CX, RD, OBS0, CAP, QQ):
            edge_copy(f, 0).wait_send()

    @pl.when(has_prev)
    def _():
        for f in (Z0, U0, U1, DPART, OBS1, OBS0, CAP, QQ):
            edge_copy(f, 1).wait_send()


def on_device(cond_x, cond_y, via_cond, via_mask, capacitance, pad_mask, observe):
    _, rows, cols = cond_x.shape
    n_ch = rows // CH
    slots = TX * TZ - 1 + TY * 4 - 1
    block = pltpu.VMEM((2, rows, cols), jnp.float32)
    ints = pltpu.VMEM((2, rows, cols), jnp.int32)
    dma = pltpu.SemaphoreType.DMA
    shape = pltpu.VMEM((2, rows, cols), jnp.float32)
    both = pl.pallas_call(
        kernel,
        out_shape=[shape, shape],
        in_specs=[pl.BlockSpec(memory_space=pl.ANY)] * 7,
        out_specs=[pl.BlockSpec(memory_space=pltpu.VMEM)] * 2,
        scratch_shapes=[
            pltpu.VMEM((2, TOP + rows, cols), jnp.float32),
            block, block, ints, block, ints,
            pltpu.VMEM((2, 2, rows, cols), jnp.float32),
            block,
            block, block, block, block,
            pltpu.VMEM((5, 2, TOP + rows + 8, cols), jnp.float32),
            pltpu.VMEM((5, 2, rows, cols), jnp.float32),
            pltpu.VMEM((rows, cols), jnp.float32),
            pltpu.VMEM((12, 2, 2, cols), jnp.float32),
            pltpu.VMEM((12, 2, 2, cols), jnp.float32),
            pltpu.VMEM((4, 8, 128), jnp.float32),
            pltpu.VMEM((2, 2, 8, 128), jnp.float32),
            pltpu.VMEM((2, slots, 8, 128), jnp.float32),
            dma((8,)),
            dma((5, 2, n_ch)), dma((5, 2, n_ch)), dma((n_ch,)), dma((n_ch,)),
            dma((12, 2)), dma((12, 2)), dma((2, slots)), dma((2, slots)),
        ],
        compiler_params=pltpu.CompilerParams(
            collective_id=0, has_side_effects=True, vmem_limit_bytes=60 * 1024 * 1024
        ),
    )(cond_x, cond_y, via_cond, via_mask, capacitance, pad_mask, observe)
    return jnp.stack(both)


def solution(mesh):
    placed = P("band", "tile", None)
    return jax.shard_map(
        on_device,
        mesh=mesh,
        in_specs=(placed,) * 6 + (P(None, "band", "tile", None),),
        out_specs=P(None, "band", "tile", None),
        check_vma=False,
    )
```

```python
import functools

import jax
import jax.numpy as jnp
from jax import lax
from jax.experimental import pallas as pl
from jax.experimental.pallas import tpu as pltpu
from jax.sharding import PartitionSpec as P

MESH = pl.DeviceIdType.MESH
PAD_CONDUCTANCE = 4.0
NB = 8
TY, TZ, TX = 2, 4, 4
CH = 8
UPWARD = 2
TOP = 8
X0, Z0, U0, Z1, U1 = range(5)
CX, DPART, OBS1, RD, OBS0, CAP, QQ = range(5, 12)


def lane_sum(p):
    parts = [p[:, k : k + 128] for k in range(0, p.shape[1], 128)]
    while len(parts) > 1:
        parts = [a + b for a, b in zip(parts[::2], parts[1::2])]
    return parts[0]


def kernel(
    cx_hbm, cy_hbm, vc_hbm, vm_hbm, cap_hbm, pm_hbm, ob_hbm, adj0, adj1,
    cx, cy, vc, vm, cap, pm, ob, vg, cxm, dg, rd, qq, field, halo, below, es, er, acc, ars, arr,
    in_sem, ps, pr, gs, gr, ess, ers, ars_sem, arr_sem,
):
    bands = lax.axis_size("band")
    tiles = lax.axis_size("tile")
    band = lax.axis_index("band")
    tile = lax.axis_index("tile")
    rows, cols = cy.shape[1], cy.shape[2]
    n_ch = rows // CH
    has_dn, has_up = band > 0, band < bands - 1
    has_prev, has_next = tile > 0, tile < tiles - 1

    def loads():
        pairs = [
            (vc_hbm, vc), (vm_hbm, vm), (cx_hbm, cx.at[:, pl.ds(TOP, rows), :]), (cy_hbm, cy), (cap_hbm, cap), (pm_hbm, pm),
            (ob_hbm.at[1], ob.at[1]), (ob_hbm.at[0], ob.at[0]),
        ]
        return [pltpu.make_async_copy(s, d, in_sem.at[k]) for k, (s, d) in enumerate(pairs)]

    ld = loads()
    for copy in ld:
        copy.start()

    tx = lax.rem(tile, TX)
    tz = lax.rem(lax.div(tile, TX), TZ)
    ty = lax.div(tile, TX * TZ)

    def peers(stage):
        if stage == 0:
            plane = tz * TX + tx
            return [(band, tile - plane + lax.rem(plane + d, TZ * TX)) for d in range(1, TZ * TX)]
        both = ty * bands + band
        out = []
        for d in range(1, TY * bands):
            other = lax.rem(both + d, TY * bands)
            out.append((lax.rem(other, bands), tile + (lax.div(other, bands) - ty) * (TX * TZ)))
        return out

    def dev(b, t):
        return {"band": b, "tile": t}

    barrier = pltpu.get_barrier_semaphore()
    known = [p for stage in range(2) for p in peers(stage)]
    for there, t in ((has_next, tile + 1), (has_prev, tile - 1)):
        @pl.when(there)
        def _():
            pl.semaphore_signal(barrier, inc=1, device_id=dev(band, t), device_id_type=MESH)
    for b, t in known:
        pl.semaphore_signal(barrier, inc=1, device_id=dev(b, t), device_id_type=MESH)

    zero_row = jnp.zeros((1, cols), jnp.float32)
    for f in range(5):
        for b in range(2):
            field[f, b, TOP - 1 : TOP, :] = zero_row
            field[f, b, TOP + rows : TOP + rows + 1, :] = zero_row

    @pl.when(jnp.logical_not(has_dn))
    def _():
        below[...] = jnp.zeros_like(below)

        @pl.loop(0, 5)
        def _(f):
            halo[f, 0] = jnp.zeros((rows, cols), jnp.float32)

    @pl.when(jnp.logical_not(has_up))
    def _():
        @pl.loop(0, 5)
        def _(f):
            halo[f, 1] = jnp.zeros((rows, cols), jnp.float32)

    acc[...] = jnp.zeros_like(acc)

    def ch(c):
        return pl.ds(pl.multiple_of(c * CH, CH), CH)

    def fch(c):
        return pl.ds(pl.multiple_of(TOP + c * CH, CH), CH)

    lane = lax.broadcasted_iota(jnp.int32, (CH, cols), 1)
    sub = lax.broadcasted_iota(jnp.int32, (CH, cols), 0)

    def row_after(here, after):
        return pltpu.roll(jnp.where(sub == 0, after, here), CH - 1, 0)

    def row_before(here, before):
        return pltpu.roll(jnp.where(sub == CH - 1, before, here), 1, 0)

    def plane_copy(f, way, c):
        return pltpu.make_async_remote_copy(
            src_ref=field.at[f, 1 - way, fch(c), :],
            dst_ref=halo.at[f, way, ch(c), :],
            send_sem=ps.at[f, way, c],
            recv_sem=pr.at[f, way, c],
            device_id=dev(band + 1 - 2 * way, tile),
            device_id_type=MESH,
        )

    def via_copy(c):
        return pltpu.make_async_remote_copy(
            src_ref=vg.at[1, ch(c), :],
            dst_ref=below.at[ch(c), :],
            send_sem=gs.at[c],
            recv_sem=gr.at[c],
            device_id=dev(band + 1, tile),
            device_id_type=MESH,
        )

    def edge_copy(f, way):
        return pltpu.make_async_remote_copy(
            src_ref=es.at[f, way],
            dst_ref=er.at[f, way],
            send_sem=ess.at[f, way],
            recv_sem=ers.at[f, way],
            device_id=dev(band, tile + 1 - 2 * way),
            device_id_type=MESH,
        )

    def send_edges(f, i, ways=(0, 1)):
        if 1 in ways:
            @pl.when(jnp.logical_and(i == 0, has_prev))
            def _():
                for b in range(2):
                    es[f, 1, b : b + 1, :] = field[f, b, TOP : TOP + 1, :]
                edge_copy(f, 1).start()
        if 0 in ways:
            @pl.when(jnp.logical_and(i == 1, has_next))
            def _():
                for b in range(2):
                    es[f, 0, b : b + 1, :] = field[f, b, TOP + rows - 1 : TOP + rows, :]
                edge_copy(f, 0).start()

    def take_edges(f, i, ways=(0, 1)):
        if 0 in ways:
            @pl.when(jnp.logical_and(i == 0, has_prev))
            def _():
                edge_copy(f, 0).wait_recv()
                for b in range(2):
                    field[f, b, TOP - 1 : TOP, :] = er[f, 0, b : b + 1, :]
        if 1 in ways and f == X0:
            @pl.when(jnp.logical_and(i == 1, has_next))
            def _():
                edge_copy(DPART, 1).wait_recv()
                edge_copy(OBS1, 1).wait_recv()
                for b in range(2):
                    r = 1.0 / (er[DPART, 1, b : b + 1, :] + cx[b, TOP + rows - 1 : TOP + rows, :])
                    er[RD, 1, b : b + 1, :] = r
                    field[X0, b, TOP + rows : TOP + rows + 1, :] = er[OBS1, 1, b : b + 1, :] * r
        elif 1 in ways:
            @pl.when(jnp.logical_and(i == 1, has_next))
            def _():
                edge_copy(f, 1).wait_recv()
                for b in range(2):
                    field[f, b, TOP + rows : TOP + rows + 1, :] = er[f, 1, b : b + 1, :]

    def send_planes(f, c, ways=(0, 1)):
        for way in ways:
            @pl.when(has_dn if way else has_up)
            def _():
                plane_copy(f, way, c).start()

    def take_planes(f, c, ways=(0, 1)):
        for way in ways:
            @pl.when(has_up if way else has_dn)
            def _():
                plane_copy(f, way, c).wait_recv()

    def order(i):
        return lax.rem(i * (n_ch - 1), n_ch)

    ld[0].wait()
    ld[1].wait()
    pl.semaphore_wait(barrier, len(known) + has_next.astype(jnp.int32) + has_prev.astype(jnp.int32))

    ld[2].wait()

    @pl.when(has_next)
    def _():
        for b in range(2):
            es[CX, 0, b : b + 1, :] = cx[b, TOP + rows - 1 : TOP + rows, :]
        edge_copy(CX, 0).start()

    @pl.loop(0, n_ch)
    def _(i):
        c = order(i)
        for b in range(2):
            keep = (band * 2 + b < NB - 1).astype(jnp.float32)
            vg[b, ch(c), :] = vc[b, ch(c), :] * vm[b, ch(c), :].astype(jnp.float32) * keep

        @pl.when(has_up)
        def _():
            via_copy(c).start()

    for b in range(2):
        cx[b, TOP - 1 : TOP, :] = zero_row
    for copy in ld[3:7]:
        copy.wait()

    def first_rows():
        for b in range(2):
            y_all = cy[b, 0:1, :]
            y_in = jnp.where(lane[0:1] == cols - 1, 0.0, y_all)
            es[DPART, 1, b : b + 1, :] = (
                cap[b, 0:1, :]
                + PAD_CONDUCTANCE * pm[b, 0:1, :].astype(jnp.float32)
                + cx[b, TOP : TOP + 1, :]
                + y_all
                + vg[b, 0:1, :]
                + pltpu.roll(y_in, 1, 1)
                + (below[0:1, :] if b == 0 else vg[0, 0:1, :])
            )
            es[OBS1, 1, b : b + 1, :] = ob[1, b, 0:1, :]
        edge_copy(DPART, 1).start()
        edge_copy(OBS1, 1).start()

    def take_row_before():
        edge_copy(CX, 0).wait_recv()
        for b in range(2):
            cx[b, TOP - 1 : TOP, :] = er[CX, 0, b : b + 1, :]

    def start_chunk(c):
        @pl.when(has_dn)
        def _():
            via_copy(c).wait_recv()

        if isinstance(c, int) and c == 0:
            @pl.when(has_prev)
            def _():
                first_rows()
                take_row_before()

        for b in range(2):
            y_all = cy[b, ch(c), :]
            y_in = jnp.where(lane == cols - 1, 0.0, y_all)
            lower = below[ch(c), :] if b == 0 else vg[0, ch(c), :]
            x_here = cx[b, fch(c), :]
            x_prev = row_before(x_here, cx[b, fch(c - 1), :])
            cxm[b, ch(c), :] = x_prev
            d = (
                cap[b, ch(c), :]
                + PAD_CONDUCTANCE * pm[b, ch(c), :].astype(jnp.float32)
                + x_here
                + y_all
                + vg[b, ch(c), :]
                + x_prev
                + pltpu.roll(y_in, 1, 1)
                + lower
            )
            r = 1.0 / d
            cy[b, ch(c), :] = y_in
            dg[b, ch(c), :] = d
            rd[b, ch(c), :] = r
            field[X0, b, fch(c), :] = ob[1, b, ch(c), :] * r
        send_planes(X0, c)

    start_chunk(n_ch - 1)

    @pl.when(has_next)
    def _():
        for b in range(2):
            es[X0, 0, b : b + 1, :] = field[X0, b, TOP + rows - 1 : TOP + rows, :]
        edge_copy(X0, 0).start()

    start_chunk(0)

    @pl.loop(2, n_ch)
    def _(i):
        start_chunk(n_ch - i)

    ld[7].wait()

    @pl.when(has_next)
    def _():
        for b in range(2):
            es[RD, 0, b : b + 1, :] = rd[b, rows - 1 : rows, :]
            es[OBS0, 0, b : b + 1, :] = ob[0, b, rows - 1 : rows, :]
            es[CAP, 0, b : b + 1, :] = cap[b, rows - 1 : rows, :]
        for f in (RD, OBS0, CAP):
            edge_copy(f, 0).start()

    @pl.when(has_prev)
    def _():
        for b in range(2):
            es[OBS0, 1, b : b + 1, :] = ob[0, b, 0:1, :]
            es[CAP, 1, b : b + 1, :] = cap[b, 0:1, :]
        for f in (OBS0, CAP):
            edge_copy(f, 1).start()

    def neighbours(f, b, c):
        v = field[f, b, fch(c), :]
        y = cy[b, ch(c), :]
        lo = halo[f, 0, ch(c), :] if b == 0 else field[f, 0, fch(c), :]
        hi = field[f, 1, fch(c), :] if b == 0 else halo[f, 1, ch(c), :]
        g_lo = below[ch(c), :] if b == 0 else vg[0, ch(c), :]
        total = (
            cx[b, fch(c), :] * row_after(v, field[f, b, fch(c + 1), :])
            + cxm[b, ch(c), :] * row_before(v, field[f, b, fch(c - 1), :])
            + vg[b, ch(c), :] * hi
            + g_lo * lo
            + y * pltpu.roll(v, cols - 1, 1)
            + pltpu.roll(y * v, 1, 1)
        )
        return v, total

    @pl.loop(0, n_ch)
    def _(i):
        c = order(i)
        take_edges(X0, i)
        take_planes(X0, c)
        for b in range(2):
            _, n = neighbours(X0, b, c)
            field[Z0, b, fch(c), :] = rd[b, ch(c), :] * n
        send_planes(Z0, c)
        send_edges(Z0, i)

    def second(fz, fu, plane_ways, edge_ways):
        @pl.loop(0, n_ch)
        def _(i):
            c = order(i)
            if fz != Z1:
                take_edges(fz, i)
            take_planes(fz, c)
            for b in range(2):
                z, n = neighbours(fz, b, c)
                dz = dg[b, ch(c), :] * z
                w = dz - n
                u = z - rd[b, ch(c), :] * n
                field[fu, b, fch(c), :] = u
                acc[0] += lane_sum(dz * z)
                acc[1] += lane_sum(w * z)
                acc[2] += lane_sum(w * u)
            plane_ways(c)
            send_edges(fu, i, edge_ways)

    def forward(f, b, c):
        v = field[f, b, fch(c), :]
        s = cx[b, fch(c), :] * row_after(v, field[f, b, fch(c + 1), :]) + cy[b, ch(c), :] * pltpu.roll(v, cols - 1, 1)
        if b == 0:
            s = s + vg[0, ch(c), :] * field[f, 1, fch(c), :]
        return v, s

    def between(f, c, low, high):
        @pl.when(jnp.logical_and(low, has_up))
        def _():
            plane_copy(f, 1, c).wait_recv()
            acc[3] += lane_sum(field[f, 1, fch(c), :] * vg[1, ch(c), :] * halo[f, 1, ch(c), :])

        @pl.when(jnp.logical_and(high, has_dn))
        def _():
            plane_copy(f, 0, c).wait_recv()
            acc[3] += lane_sum(field[f, 0, fch(c), :] * below[ch(c), :] * halo[f, 0, ch(c), :])

    sent = []

    def all_sum(k):
        quarter = lax.div(lax.broadcasted_iota(jnp.int32, (1, 128), 1), 32)
        value = jnp.zeros((1, 128), jnp.float32)
        for q in range(4):
            part = jnp.sum(acc[q], axis=0, keepdims=True)
            part = part + pltpu.roll(part, 64, 1)
            part = part + pltpu.roll(part, 32, 1)
            value = jnp.where(quarter == q, part, value)
        slot = 0
        for stage in range(2):
            ars[k, stage] = value
            copies = []
            for b, t in peers(stage):
                copies.append(
                    pltpu.make_async_remote_copy(
                        src_ref=ars.at[k, stage],
                        dst_ref=arr.at[k, slot],
                        send_sem=ars_sem.at[k, slot],
                        recv_sem=arr_sem.at[k, slot],
                        device_id=dev(b, t),
                        device_id_type=MESH,
                    )
                )
                slot += 1
            for copy in copies:
                copy.start()
            yield
            for copy in copies:
                copy.wait_recv()
            for n in range(slot - len(copies), slot):
                value = value + arr[k, n]
            sent.extend(copies)
        return [jnp.sum(jnp.where(quarter == q, value, 0.0), axis=1, keepdims=True) for q in range(4)]

    def run(gen):
        while True:
            try:
                next(gen)
            except StopIteration as end:
                return end.value

    def weights(sums):
        rz, zw, uw, edges = sums
        uau = uw - 2.0 * edges
        step0 = rz / zw
        rz_next = step0 * step0 * uw - rz
        ratio = rz_next / rz
        curve = zw - 2.0 * step0 * uw + step0 * step0 * uau - ratio * ratio * zw
        step1 = rz_next / curve
        return step0 + step1 * (1.0 + ratio), -step1 * step0

    def urgent(c):
        @pl.when(jnp.logical_and(is_low(c), has_dn))
        def _():
            plane_copy(U0, 1, c).start()

        @pl.when(jnp.logical_and(is_high(c), has_up))
        def _():
            plane_copy(U0, 0, c).start()

    def is_high(c):
        return jnp.logical_and(c >= 1, c <= UPWARD)

    def is_low(c):
        return jnp.logical_or(c == 0, c > UPWARD)

    second(Z0, U0, urgent, (0, 1))

    @pl.loop(0, n_ch)
    def _(i):
        c = order(i)

        @pl.when(jnp.logical_and(is_high(c), has_dn))
        def _():
            plane_copy(U0, 1, c).start()

        @pl.when(jnp.logical_and(is_low(c), has_up))
        def _():
            plane_copy(U0, 0, c).start()

    @pl.loop(0, n_ch)
    def _(i):
        c = order(i)
        take_edges(U0, i, (1,))
        for b in range(2):
            v, s = forward(U0, b, c)
            acc[3] += lane_sum(v * s)
        between(U0, c, is_low(c), is_high(c))

    gen = all_sum(0)
    next(gen)

    def couple(i):
        c = order(i)
        take_edges(U0, i, (0,))

        @pl.when(jnp.logical_and(is_high(c), has_up))
        def _():
            plane_copy(U0, 1, c).wait_recv()

        @pl.when(jnp.logical_and(is_low(c), has_dn))
        def _():
            plane_copy(U0, 0, c).wait_recv()

        for b in range(2):
            _, n = neighbours(U0, b, c)
            qq[b, ch(c), :] = n

        @pl.when(jnp.logical_and(i == 0, has_prev))
        def _():
            for b in range(2):
                es[QQ, 1, b : b + 1, :] = qq[b, 0:1, :]
            edge_copy(QQ, 1).start()

        @pl.when(jnp.logical_and(i == 1, has_next))
        def _():
            for b in range(2):
                es[QQ, 0, b : b + 1, :] = qq[b, rows - 1 : rows, :]
            edge_copy(QQ, 0).start()

    pl.loop(0, n_ch // 2)(couple)
    next(gen)
    pl.loop(n_ch // 2, n_ch)(couple)
    w0, w1 = weights(run(gen))
    acc[...] = jnp.zeros_like(acc)

    @pl.loop(0, n_ch)
    def _(i):
        c = order(i)
        for b in range(2):
            x = field[X0, b, fch(c), :]
            z = field[Z0, b, fch(c), :]
            u = field[U0, b, fch(c), :]
            a = x + w0 * z + w1 * u
            adj1[b, ch(c), :] = a
            inner = ob[0, b, ch(c), :] + cap[b, ch(c), :] * a + w1 * qq[b, ch(c), :]
            field[Z1, b, fch(c), :] = rd[b, ch(c), :] * inner - x + z - (w0 + w1) * u
        send_planes(Z1, c)

    def beside(way, at):
        edge_copy(QQ, way).wait_recv()
        for f in (RD, OBS0, CAP) if way == 0 else (OBS0, CAP):
            edge_copy(f, way).wait_recv()
        for b in range(2):
            x = field[X0, b, at : at + 1, :]
            z = field[Z0, b, at : at + 1, :]
            u = field[U0, b, at : at + 1, :]
            row = [er[f, way, b : b + 1, :] for f in (RD, OBS0, CAP, QQ)]
            inner = row[1] + row[2] * (x + w0 * z + w1 * u) + w1 * row[3]
            field[Z1, b, at : at + 1, :] = row[0] * inner - x + z - (w0 + w1) * u

    @pl.when(has_prev)
    def _():
        beside(0, TOP - 1)

    @pl.when(has_next)
    def _():
        beside(1, TOP + rows)

    half = n_ch // 2

    def half_planes(c):
        @pl.when(jnp.logical_and(c < half, has_dn))
        def _():
            plane_copy(U1, 1, c).start()

        @pl.when(jnp.logical_and(c >= half, has_up))
        def _():
            plane_copy(U1, 0, c).start()

    second(Z1, U1, half_planes, (1,))

    @pl.loop(0, n_ch)
    def _(i):
        c = order(i)
        take_edges(U1, i, (1,))
        for b in range(2):
            v, s = forward(U1, b, c)
            acc[3] += lane_sum(v * s)
        between(U1, c, c < half, c >= half)

    w0, w1 = weights(run(all_sum(1)))

    @pl.loop(0, n_ch)
    def _(c):
        for b in range(2):
            adj0[b, ch(c), :] = (
                adj1[b, ch(c), :] + w0 * field[Z1, b, fch(c), :] + w1 * field[U1, b, fch(c), :]
            )

    for copy in sent:
        copy.wait_send()

    @pl.loop(0, n_ch)
    def _(c):
        @pl.when(has_up)
        def _():
            via_copy(c).wait_send()

        for f in range(5):
            for way in range(2):
                sent = has_dn if way else has_up
                if f == U1:
                    sent = jnp.logical_and(sent, c < half if way else c >= half)

                @pl.when(sent)
                def _():
                    plane_copy(f, way, c).wait_send()

    @pl.when(has_next)
    def _():
        for f in (X0, Z0, U0, CX, RD, OBS0, CAP, QQ):
            edge_copy(f, 0).wait_send()

    @pl.when(has_prev)
    def _():
        for f in (Z0, U0, U1, DPART, OBS1, OBS0, CAP, QQ):
            edge_copy(f, 1).wait_send()


def on_device(cond_x, cond_y, via_cond, via_mask, capacitance, pad_mask, observe):
    _, rows, cols = cond_x.shape
    n_ch = rows // CH
    slots = TX * TZ - 1 + TY * 4 - 1
    block = pltpu.VMEM((2, rows, cols), jnp.float32)
    ints = pltpu.VMEM((2, rows, cols), jnp.int32)
    dma = pltpu.SemaphoreType.DMA
    shape = pltpu.VMEM((2, rows, cols), jnp.float32)
    both = pl.pallas_call(
        kernel,
        out_shape=[shape, shape],
        in_specs=[pl.BlockSpec(memory_space=pl.ANY)] * 7,
        out_specs=[pl.BlockSpec(memory_space=pltpu.VMEM)] * 2,
        scratch_shapes=[
            pltpu.VMEM((2, TOP + rows, cols), jnp.float32),
            block, block, ints, block, ints,
            pltpu.VMEM((2, 2, rows, cols), jnp.float32),
            block,
            block, block, block, block,
            pltpu.VMEM((5, 2, TOP + rows + 8, cols), jnp.float32),
            pltpu.VMEM((5, 2, rows, cols), jnp.float32),
            pltpu.VMEM((rows, cols), jnp.float32),
            pltpu.VMEM((12, 2, 2, cols), jnp.float32),
            pltpu.VMEM((12, 2, 2, cols), jnp.float32),
            pltpu.VMEM((4, 8, 128), jnp.float32),
            pltpu.VMEM((2, 2, 1, 128), jnp.float32),
            pltpu.VMEM((2, slots, 1, 128), jnp.float32),
            dma((8,)),
            dma((5, 2, n_ch)), dma((5, 2, n_ch)), dma((n_ch,)), dma((n_ch,)),
            dma((12, 2)), dma((12, 2)), dma((2, slots)), dma((2, slots)),
        ],
        compiler_params=pltpu.CompilerParams(
            collective_id=0, has_side_effects=True, vmem_limit_bytes=60 * 1024 * 1024
        ),
    )(cond_x, cond_y, via_cond, via_mask, capacitance, pad_mask, observe)
    return jnp.stack(both)


def solution(mesh):
    placed = P("band", "tile", None)
    return jax.shard_map(
        on_device,
        mesh=mesh,
        in_specs=(placed,) * 6 + (P(None, "band", "tile", None),),
        out_specs=P(None, "band", "tile", None),
        check_vma=False,
    )
```

```python
import functools

import jax
import jax.numpy as jnp
from jax import lax
from jax.experimental import pallas as pl
from jax.experimental.pallas import tpu as pltpu
from jax.sharding import PartitionSpec as P

MESH = pl.DeviceIdType.MESH
PAD_CONDUCTANCE = 4.0
NB = 8
TY, TZ, TX = 2, 4, 4
CH = 8
UPWARD = 2
TOP = 8
X0, Z0, U0, Z1, U1 = range(5)
CX, DPART, OBS1, RD, OBS0, CAP, QQ = range(5, 12)


def lane_sum(p):
    parts = [p[:, k : k + 128] for k in range(0, p.shape[1], 128)]
    while len(parts) > 1:
        parts = [a + b for a, b in zip(parts[::2], parts[1::2])]
    return parts[0]


def kernel(
    cx_hbm, cy_hbm, vc_hbm, vm_hbm, cap_hbm, pm_hbm, ob_hbm, adj0, adj1,
    cx, cy, vc, vm, cap, pm, ob, vg, cxm, dg, rd, qq, field, halo, below, es, er, acc, ars, arr,
    in_sem, ps, pr, gs, gr, ess, ers, ars_sem, arr_sem,
):
    bands = lax.axis_size("band")
    tiles = lax.axis_size("tile")
    band = lax.axis_index("band")
    tile = lax.axis_index("tile")
    rows, cols = cy.shape[1], cy.shape[2]
    n_ch = rows // CH
    has_dn, has_up = band > 0, band < bands - 1
    has_prev, has_next = tile > 0, tile < tiles - 1

    def loads():
        pairs = [
            (vc_hbm, vc), (vm_hbm, vm), (cx_hbm, cx.at[:, pl.ds(TOP, rows), :]), (cy_hbm, cy), (cap_hbm, cap), (pm_hbm, pm),
            (ob_hbm.at[1], ob.at[1]), (ob_hbm.at[0], ob.at[0]),
        ]
        return [pltpu.make_async_copy(s, d, in_sem.at[k]) for k, (s, d) in enumerate(pairs)]

    ld = loads()
    for copy in ld:
        copy.start()

    tx = lax.rem(tile, TX)
    tz = lax.rem(lax.div(tile, TX), TZ)
    ty = lax.div(tile, TX * TZ)

    def peers(stage):
        if stage == 0:
            plane = tz * TX + tx
            return [(band, tile - plane + lax.rem(plane + d, TZ * TX)) for d in range(1, TZ * TX)]
        both = ty * bands + band
        out = []
        for d in range(1, TY * bands):
            other = lax.rem(both + d, TY * bands)
            out.append((lax.rem(other, bands), tile + (lax.div(other, bands) - ty) * (TX * TZ)))
        return out

    def dev(b, t):
        return {"band": b, "tile": t}

    barrier = pltpu.get_barrier_semaphore()
    known = [p for stage in range(2) for p in peers(stage)]
    for there, t in ((has_next, tile + 1), (has_prev, tile - 1)):
        @pl.when(there)
        def _():
            pl.semaphore_signal(barrier, inc=1, device_id=dev(band, t), device_id_type=MESH)
    for b, t in known:
        pl.semaphore_signal(barrier, inc=1, device_id=dev(b, t), device_id_type=MESH)

    zero_row = jnp.zeros((1, cols), jnp.float32)
    for f in range(5):
        for b in range(2):
            field[f, b, TOP - 1 : TOP, :] = zero_row
            field[f, b, TOP + rows : TOP + rows + 1, :] = zero_row

    @pl.when(jnp.logical_not(has_dn))
    def _():
        below[...] = jnp.zeros_like(below)

        @pl.loop(0, 5)
        def _(f):
            halo[f, 0] = jnp.zeros((rows, cols), jnp.float32)

    @pl.when(jnp.logical_not(has_up))
    def _():
        @pl.loop(0, 5)
        def _(f):
            halo[f, 1] = jnp.zeros((rows, cols), jnp.float32)

    acc[...] = jnp.zeros_like(acc)

    def ch(c):
        return pl.ds(pl.multiple_of(c * CH, CH), CH)

    def fch(c):
        return pl.ds(pl.multiple_of(TOP + c * CH, CH), CH)

    lane = lax.broadcasted_iota(jnp.int32, (CH, cols), 1)
    sub = lax.broadcasted_iota(jnp.int32, (CH, cols), 0)

    def row_after(here, after):
        return pltpu.roll(jnp.where(sub == 0, after, here), CH - 1, 0)

    def row_before(here, before):
        return pltpu.roll(jnp.where(sub == CH - 1, before, here), 1, 0)

    def plane_copy(f, way, c):
        return pltpu.make_async_remote_copy(
            src_ref=field.at[f, 1 - way, fch(c), :],
            dst_ref=halo.at[f, way, ch(c), :],
            send_sem=ps.at[f, way, c],
            recv_sem=pr.at[f, way, c],
            device_id=dev(band + 1 - 2 * way, tile),
            device_id_type=MESH,
        )

    def via_copy(c):
        return pltpu.make_async_remote_copy(
            src_ref=vg.at[1, ch(c), :],
            dst_ref=below.at[ch(c), :],
            send_sem=gs.at[c],
            recv_sem=gr.at[c],
            device_id=dev(band + 1, tile),
            device_id_type=MESH,
        )

    def edge_copy(f, way):
        return pltpu.make_async_remote_copy(
            src_ref=es.at[f, way],
            dst_ref=er.at[f, way],
            send_sem=ess.at[f, way],
            recv_sem=ers.at[f, way],
            device_id=dev(band, tile + 1 - 2 * way),
            device_id_type=MESH,
        )

    def send_edges(f, i, ways=(0, 1)):
        if 1 in ways:
            @pl.when(jnp.logical_and(i == 0, has_prev))
            def _():
                for b in range(2):
                    es[f, 1, b : b + 1, :] = field[f, b, TOP : TOP + 1, :]
                edge_copy(f, 1).start()
        if 0 in ways:
            @pl.when(jnp.logical_and(i == 1, has_next))
            def _():
                for b in range(2):
                    es[f, 0, b : b + 1, :] = field[f, b, TOP + rows - 1 : TOP + rows, :]
                edge_copy(f, 0).start()

    def take_edges(f, i, ways=(0, 1)):
        if 0 in ways:
            @pl.when(jnp.logical_and(i == 0, has_prev))
            def _():
                edge_copy(f, 0).wait_recv()
                for b in range(2):
                    field[f, b, TOP - 1 : TOP, :] = er[f, 0, b : b + 1, :]
        if 1 in ways and f == X0:
            @pl.when(jnp.logical_and(i == 1, has_next))
            def _():
                edge_copy(DPART, 1).wait_recv()
                edge_copy(OBS1, 1).wait_recv()
                for b in range(2):
                    r = 1.0 / (er[DPART, 1, b : b + 1, :] + cx[b, TOP + rows - 1 : TOP + rows, :])
                    er[RD, 1, b : b + 1, :] = r
                    field[X0, b, TOP + rows : TOP + rows + 1, :] = er[OBS1, 1, b : b + 1, :] * r
        elif 1 in ways:
            @pl.when(jnp.logical_and(i == 1, has_next))
            def _():
                edge_copy(f, 1).wait_recv()
                for b in range(2):
                    field[f, b, TOP + rows : TOP + rows + 1, :] = er[f, 1, b : b + 1, :]

    def send_planes(f, c, ways=(0, 1)):
        for way in ways:
            @pl.when(has_dn if way else has_up)
            def _():
                plane_copy(f, way, c).start()

    def take_planes(f, c, ways=(0, 1)):
        for way in ways:
            @pl.when(has_up if way else has_dn)
            def _():
                plane_copy(f, way, c).wait_recv()

    def order(i):
        return lax.rem(i * (n_ch - 1), n_ch)

    ld[0].wait()
    ld[1].wait()
    pl.semaphore_wait(barrier, len(known) + has_next.astype(jnp.int32) + has_prev.astype(jnp.int32))

    ld[2].wait()

    @pl.when(has_next)
    def _():
        for b in range(2):
            es[CX, 0, b : b + 1, :] = cx[b, TOP + rows - 1 : TOP + rows, :]
        edge_copy(CX, 0).start()

    @pl.loop(0, n_ch)
    def _(i):
        c = order(i)
        for b in range(2):
            keep = (band * 2 + b < NB - 1).astype(jnp.float32)
            vg[b, ch(c), :] = vc[b, ch(c), :] * vm[b, ch(c), :].astype(jnp.float32) * keep

        @pl.when(has_up)
        def _():
            via_copy(c).start()

    for b in range(2):
        cx[b, TOP - 1 : TOP, :] = zero_row
    for copy in ld[3:7]:
        copy.wait()

    def first_rows():
        for b in range(2):
            y_all = cy[b, 0:1, :]
            y_in = jnp.where(lane[0:1] == cols - 1, 0.0, y_all)
            es[DPART, 1, b : b + 1, :] = (
                cap[b, 0:1, :]
                + PAD_CONDUCTANCE * pm[b, 0:1, :].astype(jnp.float32)
                + cx[b, TOP : TOP + 1, :]
                + y_all
                + vg[b, 0:1, :]
                + pltpu.roll(y_in, 1, 1)
                + (below[0:1, :] if b == 0 else vg[0, 0:1, :])
            )
            es[OBS1, 1, b : b + 1, :] = ob[1, b, 0:1, :]
        edge_copy(DPART, 1).start()
        edge_copy(OBS1, 1).start()

    def take_row_before():
        edge_copy(CX, 0).wait_recv()
        for b in range(2):
            cx[b, TOP - 1 : TOP, :] = er[CX, 0, b : b + 1, :]

    def start_chunk(c):
        @pl.when(has_dn)
        def _():
            via_copy(c).wait_recv()

        if isinstance(c, int) and c == 0:
            @pl.when(has_prev)
            def _():
                first_rows()
                take_row_before()

        for b in range(2):
            y_all = cy[b, ch(c), :]
            y_in = jnp.where(lane == cols - 1, 0.0, y_all)
            lower = below[ch(c), :] if b == 0 else vg[0, ch(c), :]
            x_here = cx[b, fch(c), :]
            x_prev = row_before(x_here, cx[b, fch(c - 1), :])
            cxm[b, ch(c), :] = x_prev
            d = (
                cap[b, ch(c), :]
                + PAD_CONDUCTANCE * pm[b, ch(c), :].astype(jnp.float32)
                + x_here
                + y_all
                + vg[b, ch(c), :]
                + x_prev
                + pltpu.roll(y_in, 1, 1)
                + lower
            )
            r = 1.0 / d
            cy[b, ch(c), :] = y_in
            dg[b, ch(c), :] = d
            rd[b, ch(c), :] = r
            field[X0, b, fch(c), :] = ob[1, b, ch(c), :] * r
        send_planes(X0, c)

    start_chunk(n_ch - 1)

    @pl.when(has_next)
    def _():
        for b in range(2):
            es[X0, 0, b : b + 1, :] = field[X0, b, TOP + rows - 1 : TOP + rows, :]
        edge_copy(X0, 0).start()

    start_chunk(0)

    @pl.loop(2, n_ch)
    def _(i):
        start_chunk(n_ch - i)

    ld[7].wait()

    @pl.when(has_next)
    def _():
        for b in range(2):
            es[RD, 0, b : b + 1, :] = rd[b, rows - 1 : rows, :]
            es[OBS0, 0, b : b + 1, :] = ob[0, b, rows - 1 : rows, :]
            es[CAP, 0, b : b + 1, :] = cap[b, rows - 1 : rows, :]
        for f in (RD, OBS0, CAP):
            edge_copy(f, 0).start()

    @pl.when(has_prev)
    def _():
        for b in range(2):
            es[OBS0, 1, b : b + 1, :] = ob[0, b, 0:1, :]
            es[CAP, 1, b : b + 1, :] = cap[b, 0:1, :]
        for f in (OBS0, CAP):
            edge_copy(f, 1).start()

    def neighbours(f, b, c):
        v = field[f, b, fch(c), :]
        y = cy[b, ch(c), :]
        lo = halo[f, 0, ch(c), :] if b == 0 else field[f, 0, fch(c), :]
        hi = field[f, 1, fch(c), :] if b == 0 else halo[f, 1, ch(c), :]
        g_lo = below[ch(c), :] if b == 0 else vg[0, ch(c), :]
        total = (
            cx[b, fch(c), :] * row_after(v, field[f, b, fch(c + 1), :])
            + cxm[b, ch(c), :] * row_before(v, field[f, b, fch(c - 1), :])
            + vg[b, ch(c), :] * hi
            + g_lo * lo
            + y * pltpu.roll(v, cols - 1, 1)
            + pltpu.roll(y * v, 1, 1)
        )
        return v, total

    @pl.loop(0, n_ch)
    def _(i):
        c = order(i)
        take_edges(X0, i)
        take_planes(X0, c)
        for b in range(2):
            _, n = neighbours(X0, b, c)
            field[Z0, b, fch(c), :] = rd[b, ch(c), :] * n
        send_planes(Z0, c)
        send_edges(Z0, i)

    def forward(f, b, c):
        v = field[f, b, fch(c), :]
        s = cx[b, fch(c), :] * row_after(v, field[f, b, fch(c + 1), :]) + cy[b, ch(c), :] * pltpu.roll(v, cols - 1, 1)
        if b == 0:
            s = s + vg[0, ch(c), :] * field[f, 1, fch(c), :]
        return v, s

    def between(f, c, low, high):
        @pl.when(jnp.logical_and(low, has_up))
        def _():
            plane_copy(f, 1, c).wait_recv()
            acc[3] += lane_sum(field[f, 1, fch(c), :] * vg[1, ch(c), :] * halo[f, 1, ch(c), :])

        @pl.when(jnp.logical_and(high, has_dn))
        def _():
            plane_copy(f, 0, c).wait_recv()
            acc[3] += lane_sum(field[f, 0, fch(c), :] * below[ch(c), :] * halo[f, 0, ch(c), :])

    def inside(f, c):
        for b in range(2):
            v, s = forward(f, b, c)
            acc[3] += lane_sum(v * s)

    def second(fz, fu, plane_ways, edge_ways):
        @pl.loop(0, n_ch)
        def _(i):
            c = order(i)
            if fz != Z1:
                take_edges(fz, i)
            take_planes(fz, c)
            for b in range(2):
                z, n = neighbours(fz, b, c)
                dz = dg[b, ch(c), :] * z
                w = dz - n
                u = z - rd[b, ch(c), :] * n
                field[fu, b, fch(c), :] = u
                acc[0] += lane_sum(dz * z)
                acc[1] += lane_sum(w * z)
                acc[2] += lane_sum(w * u)
            plane_ways(c)
            send_edges(fu, i, edge_ways)

            @pl.when(i >= 2)
            def _():
                inside(fu, c)

    def rest(fu, low, high):
        inside(fu, 0)
        take_edges(fu, 1, (1,))
        inside(fu, n_ch - 1)

        @pl.loop(0, n_ch)
        def _(i):
            c = order(i)
            between(fu, c, low(c), high(c))

    sent = []

    def all_sum(k):
        quarter = lax.div(lax.broadcasted_iota(jnp.int32, (1, 128), 1), 32)
        value = jnp.zeros((1, 128), jnp.float32)
        for q in range(4):
            part = jnp.sum(acc[q], axis=0, keepdims=True)
            part = part + pltpu.roll(part, 64, 1)
            part = part + pltpu.roll(part, 32, 1)
            value = jnp.where(quarter == q, part, value)
        slot = 0
        for stage in range(2):
            ars[k, stage] = value
            copies = []
            for b, t in peers(stage):
                copies.append(
                    pltpu.make_async_remote_copy(
                        src_ref=ars.at[k, stage],
                        dst_ref=arr.at[k, slot],
                        send_sem=ars_sem.at[k, slot],
                        recv_sem=arr_sem.at[k, slot],
                        device_id=dev(b, t),
                        device_id_type=MESH,
                    )
                )
                slot += 1
            for copy in copies:
                copy.start()
            yield
            for copy in copies:
                copy.wait_recv()
            for n in range(slot - len(copies), slot):
                value = value + arr[k, n]
            sent.extend(copies)
        return [jnp.sum(jnp.where(quarter == q, value, 0.0), axis=1, keepdims=True) for q in range(4)]

    def run(gen):
        while True:
            try:
                next(gen)
            except StopIteration as end:
                return end.value

    def weights(sums):
        rz, zw, uw, edges = sums
        uau = uw - 2.0 * edges
        step0 = rz / zw
        rz_next = step0 * step0 * uw - rz
        ratio = rz_next / rz
        curve = zw - 2.0 * step0 * uw + step0 * step0 * uau - ratio * ratio * zw
        step1 = rz_next / curve
        return step0 + step1 * (1.0 + ratio), -step1 * step0

    def urgent(c):
        @pl.when(jnp.logical_and(is_low(c), has_dn))
        def _():
            plane_copy(U0, 1, c).start()

        @pl.when(jnp.logical_and(is_high(c), has_up))
        def _():
            plane_copy(U0, 0, c).start()

    def is_high(c):
        return jnp.logical_and(c >= 1, c <= UPWARD)

    def is_low(c):
        return jnp.logical_or(c == 0, c > UPWARD)

    second(Z0, U0, urgent, (0, 1))

    @pl.loop(0, n_ch)
    def _(i):
        c = order(i)

        @pl.when(jnp.logical_and(is_high(c), has_dn))
        def _():
            plane_copy(U0, 1, c).start()

        @pl.when(jnp.logical_and(is_low(c), has_up))
        def _():
            plane_copy(U0, 0, c).start()

    rest(U0, is_low, is_high)

    gen = all_sum(0)
    next(gen)

    def couple(i):
        c = order(i)
        take_edges(U0, i, (0,))

        @pl.when(jnp.logical_and(is_high(c), has_up))
        def _():
            plane_copy(U0, 1, c).wait_recv()

        @pl.when(jnp.logical_and(is_low(c), has_dn))
        def _():
            plane_copy(U0, 0, c).wait_recv()

        for b in range(2):
            _, n = neighbours(U0, b, c)
            qq[b, ch(c), :] = n

        @pl.when(jnp.logical_and(i == 0, has_prev))
        def _():
            for b in range(2):
                es[QQ, 1, b : b + 1, :] = qq[b, 0:1, :]
            edge_copy(QQ, 1).start()

        @pl.when(jnp.logical_and(i == 1, has_next))
        def _():
            for b in range(2):
                es[QQ, 0, b : b + 1, :] = qq[b, rows - 1 : rows, :]
            edge_copy(QQ, 0).start()

    next(gen)
    pl.loop(0, n_ch)(couple)
    w0, w1 = weights(run(gen))
    acc[...] = jnp.zeros_like(acc)

    @pl.loop(0, n_ch)
    def _(i):
        c = order(i)
        for b in range(2):
            x = field[X0, b, fch(c), :]
            z = field[Z0, b, fch(c), :]
            u = field[U0, b, fch(c), :]
            a = x + w0 * z + w1 * u
            adj1[b, ch(c), :] = a
            inner = ob[0, b, ch(c), :] + cap[b, ch(c), :] * a + w1 * qq[b, ch(c), :]
            field[Z1, b, fch(c), :] = rd[b, ch(c), :] * inner - x + z - (w0 + w1) * u
        send_planes(Z1, c)

    def beside(way, at):
        edge_copy(QQ, way).wait_recv()
        for f in (RD, OBS0, CAP) if way == 0 else (OBS0, CAP):
            edge_copy(f, way).wait_recv()
        for b in range(2):
            x = field[X0, b, at : at + 1, :]
            z = field[Z0, b, at : at + 1, :]
            u = field[U0, b, at : at + 1, :]
            row = [er[f, way, b : b + 1, :] for f in (RD, OBS0, CAP, QQ)]
            inner = row[1] + row[2] * (x + w0 * z + w1 * u) + w1 * row[3]
            field[Z1, b, at : at + 1, :] = row[0] * inner - x + z - (w0 + w1) * u

    @pl.when(has_prev)
    def _():
        beside(0, TOP - 1)

    @pl.when(has_next)
    def _():
        beside(1, TOP + rows)

    half = n_ch // 2

    def half_planes(c):
        @pl.when(jnp.logical_and(c < half, has_dn))
        def _():
            plane_copy(U1, 1, c).start()

        @pl.when(jnp.logical_and(c >= half, has_up))
        def _():
            plane_copy(U1, 0, c).start()

    second(Z1, U1, half_planes, (1,))

    rest(U1, lambda c: c < half, lambda c: c >= half)

    w0, w1 = weights(run(all_sum(1)))

    @pl.loop(0, n_ch)
    def _(c):
        for b in range(2):
            adj0[b, ch(c), :] = (
                adj1[b, ch(c), :] + w0 * field[Z1, b, fch(c), :] + w1 * field[U1, b, fch(c), :]
            )

    for copy in sent:
        copy.wait_send()

    @pl.loop(0, n_ch)
    def _(c):
        @pl.when(has_up)
        def _():
            via_copy(c).wait_send()

        for f in range(5):
            for way in range(2):
                sent = has_dn if way else has_up
                if f == U1:
                    sent = jnp.logical_and(sent, c < half if way else c >= half)

                @pl.when(sent)
                def _():
                    plane_copy(f, way, c).wait_send()

    @pl.when(has_next)
    def _():
        for f in (X0, Z0, U0, CX, RD, OBS0, CAP, QQ):
            edge_copy(f, 0).wait_send()

    @pl.when(has_prev)
    def _():
        for f in (Z0, U0, U1, DPART, OBS1, OBS0, CAP, QQ):
            edge_copy(f, 1).wait_send()


def on_device(cond_x, cond_y, via_cond, via_mask, capacitance, pad_mask, observe):
    _, rows, cols = cond_x.shape
    n_ch = rows // CH
    slots = TX * TZ - 1 + TY * 4 - 1
    block = pltpu.VMEM((2, rows, cols), jnp.float32)
    ints = pltpu.VMEM((2, rows, cols), jnp.int32)
    dma = pltpu.SemaphoreType.DMA
    shape = pltpu.VMEM((2, rows, cols), jnp.float32)
    both = pl.pallas_call(
        kernel,
        out_shape=[shape, shape],
        in_specs=[pl.BlockSpec(memory_space=pl.ANY)] * 7,
        out_specs=[pl.BlockSpec(memory_space=pltpu.VMEM)] * 2,
        scratch_shapes=[
            pltpu.VMEM((2, TOP + rows, cols), jnp.float32),
            block, block, ints, block, ints,
            pltpu.VMEM((2, 2, rows, cols), jnp.float32),
            block,
            block, block, block, block,
            pltpu.VMEM((5, 2, TOP + rows + 8, cols), jnp.float32),
            pltpu.VMEM((5, 2, rows, cols), jnp.float32),
            pltpu.VMEM((rows, cols), jnp.float32),
            pltpu.VMEM((12, 2, 2, cols), jnp.float32),
            pltpu.VMEM((12, 2, 2, cols), jnp.float32),
            pltpu.VMEM((4, 8, 128), jnp.float32),
            pltpu.VMEM((2, 2, 1, 128), jnp.float32),
            pltpu.VMEM((2, slots, 1, 128), jnp.float32),
            dma((8,)),
            dma((5, 2, n_ch)), dma((5, 2, n_ch)), dma((n_ch,)), dma((n_ch,)),
            dma((12, 2)), dma((12, 2)), dma((2, slots)), dma((2, slots)),
        ],
        compiler_params=pltpu.CompilerParams(
            collective_id=0, has_side_effects=True, vmem_limit_bytes=60 * 1024 * 1024
        ),
    )(cond_x, cond_y, via_cond, via_mask, capacitance, pad_mask, observe)
    return jnp.stack(both)


def solution(mesh):
    placed = P("band", "tile", None)
    return jax.shard_map(
        on_device,
        mesh=mesh,
        in_specs=(placed,) * 6 + (P(None, "band", "tile", None),),
        out_specs=P(None, "band", "tile", None),
        check_vma=False,
    )
```

```python
import functools

import jax
import jax.numpy as jnp
from jax import lax
from jax.experimental import pallas as pl
from jax.experimental.pallas import tpu as pltpu
from jax.sharding import PartitionSpec as P

MESH = pl.DeviceIdType.MESH
PAD_CONDUCTANCE = 4.0
NB = 8
TY, TZ, TX = 2, 4, 4
CH = 8
UPWARD = 2
TOP = 8
X0, Z0, U0, Z1, U1 = range(5)
CX, DPART, OBS1, RD, OBS0, CAP, QQ = range(5, 12)


def lane_sum(p):
    parts = [p[:, k : k + 128] for k in range(0, p.shape[1], 128)]
    while len(parts) > 1:
        parts = [a + b for a, b in zip(parts[::2], parts[1::2])]
    return parts[0]


def kernel(
    cx_hbm, cy_hbm, vc_hbm, vm_hbm, cap_hbm, pm_hbm, ob_hbm, adj1, z_out, u_out, w_out,
    cx, cy, vc, vm, cap, pm, ob, vg, cxm, dg, rd, qq, field, halo, below, es, er, acc, ars, arr,
    in_sem, ps, pr, gs, gr, ess, ers, ars_sem, arr_sem,
):
    bands = lax.axis_size("band")
    tiles = lax.axis_size("tile")
    band = lax.axis_index("band")
    tile = lax.axis_index("tile")
    rows, cols = cy.shape[1], cy.shape[2]
    n_ch = rows // CH
    has_dn, has_up = band > 0, band < bands - 1
    has_prev, has_next = tile > 0, tile < tiles - 1

    def loads():
        pairs = [
            (vc_hbm, vc), (vm_hbm, vm), (cx_hbm, cx.at[:, pl.ds(TOP, rows), :]), (cy_hbm, cy), (cap_hbm, cap), (pm_hbm, pm),
            (ob_hbm.at[1], ob.at[1]), (ob_hbm.at[0], ob.at[0]),
        ]
        return [pltpu.make_async_copy(s, d, in_sem.at[k]) for k, (s, d) in enumerate(pairs)]

    ld = loads()
    for copy in ld:
        copy.start()

    tx = lax.rem(tile, TX)
    tz = lax.rem(lax.div(tile, TX), TZ)
    ty = lax.div(tile, TX * TZ)

    def peers(stage):
        if stage == 0:
            plane = tz * TX + tx
            return [(band, tile - plane + lax.rem(plane + d, TZ * TX)) for d in range(1, TZ * TX)]
        both = ty * bands + band
        out = []
        for d in range(1, TY * bands):
            other = lax.rem(both + d, TY * bands)
            out.append((lax.rem(other, bands), tile + (lax.div(other, bands) - ty) * (TX * TZ)))
        return out

    def dev(b, t):
        return {"band": b, "tile": t}

    barrier = pltpu.get_barrier_semaphore()
    known = [p for stage in range(2) for p in peers(stage)]
    for there, t in ((has_next, tile + 1), (has_prev, tile - 1)):
        @pl.when(there)
        def _():
            pl.semaphore_signal(barrier, inc=1, device_id=dev(band, t), device_id_type=MESH)
    for b, t in known:
        pl.semaphore_signal(barrier, inc=1, device_id=dev(b, t), device_id_type=MESH)

    zero_row = jnp.zeros((1, cols), jnp.float32)
    for f in range(5):
        for b in range(2):
            field[f, b, TOP - 1 : TOP, :] = zero_row
            field[f, b, TOP + rows : TOP + rows + 1, :] = zero_row

    @pl.when(jnp.logical_not(has_dn))
    def _():
        below[...] = jnp.zeros_like(below)

        @pl.loop(0, 5)
        def _(f):
            halo[f, 0] = jnp.zeros((rows, cols), jnp.float32)

    @pl.when(jnp.logical_not(has_up))
    def _():
        @pl.loop(0, 5)
        def _(f):
            halo[f, 1] = jnp.zeros((rows, cols), jnp.float32)

    acc[...] = jnp.zeros_like(acc)

    def ch(c):
        return pl.ds(pl.multiple_of(c * CH, CH), CH)

    def fch(c):
        return pl.ds(pl.multiple_of(TOP + c * CH, CH), CH)

    lane = lax.broadcasted_iota(jnp.int32, (CH, cols), 1)
    sub = lax.broadcasted_iota(jnp.int32, (CH, cols), 0)

    def row_after(here, after):
        return pltpu.roll(jnp.where(sub == 0, after, here), CH - 1, 0)

    def row_before(here, before):
        return pltpu.roll(jnp.where(sub == CH - 1, before, here), 1, 0)

    def plane_copy(f, way, c):
        return pltpu.make_async_remote_copy(
            src_ref=field.at[f, 1 - way, fch(c), :],
            dst_ref=halo.at[f, way, ch(c), :],
            send_sem=ps.at[f, way, c],
            recv_sem=pr.at[f, way, c],
            device_id=dev(band + 1 - 2 * way, tile),
            device_id_type=MESH,
        )

    def via_copy(c):
        return pltpu.make_async_remote_copy(
            src_ref=vg.at[1, ch(c), :],
            dst_ref=below.at[ch(c), :],
            send_sem=gs.at[c],
            recv_sem=gr.at[c],
            device_id=dev(band + 1, tile),
            device_id_type=MESH,
        )

    def edge_copy(f, way):
        return pltpu.make_async_remote_copy(
            src_ref=es.at[f, way],
            dst_ref=er.at[f, way],
            send_sem=ess.at[f, way],
            recv_sem=ers.at[f, way],
            device_id=dev(band, tile + 1 - 2 * way),
            device_id_type=MESH,
        )

    def send_edges(f, i, ways=(0, 1)):
        if 1 in ways:
            @pl.when(jnp.logical_and(i == 0, has_prev))
            def _():
                for b in range(2):
                    es[f, 1, b : b + 1, :] = field[f, b, TOP : TOP + 1, :]
                edge_copy(f, 1).start()
        if 0 in ways:
            @pl.when(jnp.logical_and(i == 1, has_next))
            def _():
                for b in range(2):
                    es[f, 0, b : b + 1, :] = field[f, b, TOP + rows - 1 : TOP + rows, :]
                edge_copy(f, 0).start()

    def take_edges(f, i, ways=(0, 1)):
        if 0 in ways:
            @pl.when(jnp.logical_and(i == 0, has_prev))
            def _():
                edge_copy(f, 0).wait_recv()
                for b in range(2):
                    field[f, b, TOP - 1 : TOP, :] = er[f, 0, b : b + 1, :]
        if 1 in ways and f == X0:
            @pl.when(jnp.logical_and(i == 1, has_next))
            def _():
                edge_copy(DPART, 1).wait_recv()
                edge_copy(OBS1, 1).wait_recv()
                for b in range(2):
                    r = 1.0 / (er[DPART, 1, b : b + 1, :] + cx[b, TOP + rows - 1 : TOP + rows, :])
                    er[RD, 1, b : b + 1, :] = r
                    field[X0, b, TOP + rows : TOP + rows + 1, :] = er[OBS1, 1, b : b + 1, :] * r
        elif 1 in ways:
            @pl.when(jnp.logical_and(i == 1, has_next))
            def _():
                edge_copy(f, 1).wait_recv()
                for b in range(2):
                    field[f, b, TOP + rows : TOP + rows + 1, :] = er[f, 1, b : b + 1, :]

    def send_planes(f, c, ways=(0, 1)):
        for way in ways:
            @pl.when(has_dn if way else has_up)
            def _():
                plane_copy(f, way, c).start()

    def take_planes(f, c, ways=(0, 1)):
        for way in ways:
            @pl.when(has_up if way else has_dn)
            def _():
                plane_copy(f, way, c).wait_recv()

    def order(i):
        return lax.rem(i * (n_ch - 1), n_ch)

    ld[0].wait()
    ld[1].wait()
    pl.semaphore_wait(barrier, len(known) + has_next.astype(jnp.int32) + has_prev.astype(jnp.int32))

    ld[2].wait()

    @pl.when(has_next)
    def _():
        for b in range(2):
            es[CX, 0, b : b + 1, :] = cx[b, TOP + rows - 1 : TOP + rows, :]
        edge_copy(CX, 0).start()

    @pl.loop(0, n_ch)
    def _(i):
        c = order(i)
        for b in range(2):
            keep = (band * 2 + b < NB - 1).astype(jnp.float32)
            vg[b, ch(c), :] = vc[b, ch(c), :] * vm[b, ch(c), :].astype(jnp.float32) * keep

        @pl.when(has_up)
        def _():
            via_copy(c).start()

    for b in range(2):
        cx[b, TOP - 1 : TOP, :] = zero_row
    for copy in ld[3:7]:
        copy.wait()

    def first_rows():
        for b in range(2):
            y_all = cy[b, 0:1, :]
            y_in = jnp.where(lane[0:1] == cols - 1, 0.0, y_all)
            es[DPART, 1, b : b + 1, :] = (
                cap[b, 0:1, :]
                + PAD_CONDUCTANCE * pm[b, 0:1, :].astype(jnp.float32)
                + cx[b, TOP : TOP + 1, :]
                + y_all
                + vg[b, 0:1, :]
                + pltpu.roll(y_in, 1, 1)
                + (below[0:1, :] if b == 0 else vg[0, 0:1, :])
            )
            es[OBS1, 1, b : b + 1, :] = ob[1, b, 0:1, :]
        edge_copy(DPART, 1).start()
        edge_copy(OBS1, 1).start()

    def take_row_before():
        edge_copy(CX, 0).wait_recv()
        for b in range(2):
            cx[b, TOP - 1 : TOP, :] = er[CX, 0, b : b + 1, :]

    def start_chunk(c):
        @pl.when(has_dn)
        def _():
            via_copy(c).wait_recv()

        if isinstance(c, int) and c == 0:
            @pl.when(has_prev)
            def _():
                first_rows()
                take_row_before()

        for b in range(2):
            y_all = cy[b, ch(c), :]
            y_in = jnp.where(lane == cols - 1, 0.0, y_all)
            lower = below[ch(c), :] if b == 0 else vg[0, ch(c), :]
            x_here = cx[b, fch(c), :]
            x_prev = row_before(x_here, cx[b, fch(c - 1), :])
            cxm[b, ch(c), :] = x_prev
            d = (
                cap[b, ch(c), :]
                + PAD_CONDUCTANCE * pm[b, ch(c), :].astype(jnp.float32)
                + x_here
                + y_all
                + vg[b, ch(c), :]
                + x_prev
                + pltpu.roll(y_in, 1, 1)
                + lower
            )
            r = 1.0 / d
            cy[b, ch(c), :] = y_in
            dg[b, ch(c), :] = d
            rd[b, ch(c), :] = r
            field[X0, b, fch(c), :] = ob[1, b, ch(c), :] * r
        send_planes(X0, c)

    start_chunk(n_ch - 1)

    @pl.when(has_next)
    def _():
        for b in range(2):
            es[X0, 0, b : b + 1, :] = field[X0, b, TOP + rows - 1 : TOP + rows, :]
        edge_copy(X0, 0).start()

    start_chunk(0)

    @pl.loop(2, n_ch)
    def _(i):
        start_chunk(n_ch - i)

    ld[7].wait()

    @pl.when(has_next)
    def _():
        for b in range(2):
            es[RD, 0, b : b + 1, :] = rd[b, rows - 1 : rows, :]
            es[OBS0, 0, b : b + 1, :] = ob[0, b, rows - 1 : rows, :]
            es[CAP, 0, b : b + 1, :] = cap[b, rows - 1 : rows, :]
        for f in (RD, OBS0, CAP):
            edge_copy(f, 0).start()

    @pl.when(has_prev)
    def _():
        for b in range(2):
            es[OBS0, 1, b : b + 1, :] = ob[0, b, 0:1, :]
            es[CAP, 1, b : b + 1, :] = cap[b, 0:1, :]
        for f in (OBS0, CAP):
            edge_copy(f, 1).start()

    def neighbours(f, b, c):
        v = field[f, b, fch(c), :]
        y = cy[b, ch(c), :]
        lo = halo[f, 0, ch(c), :] if b == 0 else field[f, 0, fch(c), :]
        hi = field[f, 1, fch(c), :] if b == 0 else halo[f, 1, ch(c), :]
        g_lo = below[ch(c), :] if b == 0 else vg[0, ch(c), :]
        total = (
            cx[b, fch(c), :] * row_after(v, field[f, b, fch(c + 1), :])
            + cxm[b, ch(c), :] * row_before(v, field[f, b, fch(c - 1), :])
            + vg[b, ch(c), :] * hi
            + g_lo * lo
            + y * pltpu.roll(v, cols - 1, 1)
            + pltpu.roll(y * v, 1, 1)
        )
        return v, total

    @pl.loop(0, n_ch)
    def _(i):
        c = order(i)
        take_edges(X0, i)
        take_planes(X0, c)
        for b in range(2):
            _, n = neighbours(X0, b, c)
            field[Z0, b, fch(c), :] = rd[b, ch(c), :] * n
        send_planes(Z0, c)
        send_edges(Z0, i)

    def forward(f, b, c):
        v = field[f, b, fch(c), :]
        s = cx[b, fch(c), :] * row_after(v, field[f, b, fch(c + 1), :]) + cy[b, ch(c), :] * pltpu.roll(v, cols - 1, 1)
        if b == 0:
            s = s + vg[0, ch(c), :] * field[f, 1, fch(c), :]
        return v, s

    def between(f, c, low, high):
        @pl.when(jnp.logical_and(low, has_up))
        def _():
            plane_copy(f, 1, c).wait_recv()
            acc[3] += lane_sum(field[f, 1, fch(c), :] * vg[1, ch(c), :] * halo[f, 1, ch(c), :])

        @pl.when(jnp.logical_and(high, has_dn))
        def _():
            plane_copy(f, 0, c).wait_recv()
            acc[3] += lane_sum(field[f, 0, fch(c), :] * below[ch(c), :] * halo[f, 0, ch(c), :])

    def inside(f, c):
        for b in range(2):
            v, s = forward(f, b, c)
            acc[3] += lane_sum(v * s)

    def second(fz, fu, plane_ways, edge_ways):
        @pl.loop(0, n_ch)
        def _(i):
            c = order(i)
            if fz != Z1:
                take_edges(fz, i)
            take_planes(fz, c)
            for b in range(2):
                z, n = neighbours(fz, b, c)
                dz = dg[b, ch(c), :] * z
                w = dz - n
                u = z - rd[b, ch(c), :] * n
                field[fu, b, fch(c), :] = u
                if fu == U1:
                    u_out[b, ch(c), :] = u
                acc[0] += lane_sum(dz * z)
                acc[1] += lane_sum(w * z)
                acc[2] += lane_sum(w * u)
            plane_ways(c)
            send_edges(fu, i, edge_ways)

            @pl.when(i >= 2)
            def _():
                inside(fu, c)

    def rest(fu, low, high):
        inside(fu, 0)
        take_edges(fu, 1, (1,))
        inside(fu, n_ch - 1)

        @pl.loop(0, n_ch)
        def _(i):
            c = order(i)
            between(fu, c, low(c), high(c))

    sent = []

    def all_sum(k):
        quarter = lax.div(lax.broadcasted_iota(jnp.int32, (1, 128), 1), 32)
        value = jnp.zeros((1, 128), jnp.float32)
        for q in range(4):
            part = jnp.sum(acc[q], axis=0, keepdims=True)
            part = part + pltpu.roll(part, 64, 1)
            part = part + pltpu.roll(part, 32, 1)
            value = jnp.where(quarter == q, part, value)
        slot = 0
        for stage in range(2):
            ars[k, stage] = value
            copies = []
            for b, t in peers(stage):
                copies.append(
                    pltpu.make_async_remote_copy(
                        src_ref=ars.at[k, stage],
                        dst_ref=arr.at[k, slot],
                        send_sem=ars_sem.at[k, slot],
                        recv_sem=arr_sem.at[k, slot],
                        device_id=dev(b, t),
                        device_id_type=MESH,
                    )
                )
                slot += 1
            for copy in copies:
                copy.start()
            yield
            for copy in copies:
                copy.wait_recv()
            for n in range(slot - len(copies), slot):
                value = value + arr[k, n]
            sent.extend(copies)
        return [jnp.sum(jnp.where(quarter == q, value, 0.0), axis=1, keepdims=True) for q in range(4)]

    def run(gen):
        while True:
            try:
                next(gen)
            except StopIteration as end:
                return end.value

    def weights(sums):
        rz, zw, uw, edges = sums
        uau = uw - 2.0 * edges
        step0 = rz / zw
        rz_next = step0 * step0 * uw - rz
        ratio = rz_next / rz
        curve = zw - 2.0 * step0 * uw + step0 * step0 * uau - ratio * ratio * zw
        step1 = rz_next / curve
        return step0 + step1 * (1.0 + ratio), -step1 * step0

    def urgent(c):
        @pl.when(jnp.logical_and(is_low(c), has_dn))
        def _():
            plane_copy(U0, 1, c).start()

        @pl.when(jnp.logical_and(is_high(c), has_up))
        def _():
            plane_copy(U0, 0, c).start()

    def is_high(c):
        return jnp.logical_and(c >= 1, c <= UPWARD)

    def is_low(c):
        return jnp.logical_or(c == 0, c > UPWARD)

    second(Z0, U0, urgent, (0, 1))

    @pl.loop(0, n_ch)
    def _(i):
        c = order(i)

        @pl.when(jnp.logical_and(is_high(c), has_dn))
        def _():
            plane_copy(U0, 1, c).start()

        @pl.when(jnp.logical_and(is_low(c), has_up))
        def _():
            plane_copy(U0, 0, c).start()

    rest(U0, is_low, is_high)

    gen = all_sum(0)
    next(gen)

    def couple(i):
        c = order(i)
        take_edges(U0, i, (0,))

        @pl.when(jnp.logical_and(is_high(c), has_up))
        def _():
            plane_copy(U0, 1, c).wait_recv()

        @pl.when(jnp.logical_and(is_low(c), has_dn))
        def _():
            plane_copy(U0, 0, c).wait_recv()

        for b in range(2):
            _, n = neighbours(U0, b, c)
            qq[b, ch(c), :] = n

        @pl.when(jnp.logical_and(i == 0, has_prev))
        def _():
            for b in range(2):
                es[QQ, 1, b : b + 1, :] = qq[b, 0:1, :]
            edge_copy(QQ, 1).start()

        @pl.when(jnp.logical_and(i == 1, has_next))
        def _():
            for b in range(2):
                es[QQ, 0, b : b + 1, :] = qq[b, rows - 1 : rows, :]
            edge_copy(QQ, 0).start()

    next(gen)
    pl.loop(0, n_ch)(couple)
    w0, w1 = weights(run(gen))
    acc[...] = jnp.zeros_like(acc)

    @pl.loop(0, n_ch)
    def _(i):
        c = order(i)
        for b in range(2):
            x = field[X0, b, fch(c), :]
            z = field[Z0, b, fch(c), :]
            u = field[U0, b, fch(c), :]
            a = x + w0 * z + w1 * u
            adj1[b, ch(c), :] = a
            inner = ob[0, b, ch(c), :] + cap[b, ch(c), :] * a + w1 * qq[b, ch(c), :]
            z_new = rd[b, ch(c), :] * inner - x + z - (w0 + w1) * u
            field[Z1, b, fch(c), :] = z_new
            z_out[b, ch(c), :] = z_new
        send_planes(Z1, c)

    def beside(way, at):
        edge_copy(QQ, way).wait_recv()
        for f in (RD, OBS0, CAP) if way == 0 else (OBS0, CAP):
            edge_copy(f, way).wait_recv()
        for b in range(2):
            x = field[X0, b, at : at + 1, :]
            z = field[Z0, b, at : at + 1, :]
            u = field[U0, b, at : at + 1, :]
            row = [er[f, way, b : b + 1, :] for f in (RD, OBS0, CAP, QQ)]
            inner = row[1] + row[2] * (x + w0 * z + w1 * u) + w1 * row[3]
            field[Z1, b, at : at + 1, :] = row[0] * inner - x + z - (w0 + w1) * u

    @pl.when(has_prev)
    def _():
        beside(0, TOP - 1)

    @pl.when(has_next)
    def _():
        beside(1, TOP + rows)

    half = n_ch // 2

    def half_planes(c):
        @pl.when(jnp.logical_and(c < half, has_dn))
        def _():
            plane_copy(U1, 1, c).start()

        @pl.when(jnp.logical_and(c >= half, has_up))
        def _():
            plane_copy(U1, 0, c).start()

    second(Z1, U1, half_planes, (1,))

    rest(U1, lambda c: c < half, lambda c: c >= half)

    w0, w1 = weights(run(all_sum(1)))
    w_out[0:1, :] = jnp.broadcast_to(w0, (1, 128))
    w_out[1:2, :] = jnp.broadcast_to(w1, (1, 128))

    for copy in sent:
        copy.wait_send()

    @pl.loop(0, n_ch)
    def _(c):
        @pl.when(has_up)
        def _():
            via_copy(c).wait_send()

        for f in range(5):
            for way in range(2):
                sent = has_dn if way else has_up
                if f == U1:
                    sent = jnp.logical_and(sent, c < half if way else c >= half)

                @pl.when(sent)
                def _():
                    plane_copy(f, way, c).wait_send()

    @pl.when(has_next)
    def _():
        for f in (X0, Z0, U0, CX, RD, OBS0, CAP, QQ):
            edge_copy(f, 0).wait_send()

    @pl.when(has_prev)
    def _():
        for f in (Z0, U0, U1, DPART, OBS1, OBS0, CAP, QQ):
            edge_copy(f, 1).wait_send()


PIECES = 4


def finish(adj1, z, u, w, out, adj0, sem):
    copies = [pltpu.make_async_copy(adj1, out.at[1], sem.at[PIECES])]
    copies[0].start()
    w0, w1 = w[0:1, 0:1], w[1:2, 0:1]
    size = adj1.shape[1] // PIECES
    for n in range(PIECES):
        part = pl.ds(n * size, size)
        for b in range(2):
            adj0[b, part, :] = adj1[b, part, :] + w0 * z[b, part, :] + w1 * u[b, part, :]
        copies.append(pltpu.make_async_copy(adj0.at[:, part, :], out.at[0, :, part, :], sem.at[n]))
        copies[-1].start()
    for copy in copies:
        copy.wait()


def on_device(cond_x, cond_y, via_cond, via_mask, capacitance, pad_mask, observe):
    _, rows, cols = cond_x.shape
    n_ch = rows // CH
    slots = TX * TZ - 1 + TY * 4 - 1
    block = pltpu.VMEM((2, rows, cols), jnp.float32)
    ints = pltpu.VMEM((2, rows, cols), jnp.int32)
    dma = pltpu.SemaphoreType.DMA
    shape = pltpu.VMEM((2, rows, cols), jnp.float32)
    both = pl.pallas_call(
        kernel,
        out_shape=[shape, shape, shape, pltpu.VMEM((8, 128), jnp.float32)],
        in_specs=[pl.BlockSpec(memory_space=pl.ANY)] * 7,
        out_specs=[pl.BlockSpec(memory_space=pltpu.VMEM)] * 4,
        scratch_shapes=[
            pltpu.VMEM((2, TOP + rows, cols), jnp.float32),
            block, block, ints, block, ints,
            pltpu.VMEM((2, 2, rows, cols), jnp.float32),
            block,
            block, block, block, block,
            pltpu.VMEM((5, 2, TOP + rows + 8, cols), jnp.float32),
            pltpu.VMEM((5, 2, rows, cols), jnp.float32),
            pltpu.VMEM((rows, cols), jnp.float32),
            pltpu.VMEM((12, 2, 2, cols), jnp.float32),
            pltpu.VMEM((12, 2, 2, cols), jnp.float32),
            pltpu.VMEM((4, 8, 128), jnp.float32),
            pltpu.VMEM((2, 2, 1, 128), jnp.float32),
            pltpu.VMEM((2, slots, 1, 128), jnp.float32),
            dma((8,)),
            dma((5, 2, n_ch)), dma((5, 2, n_ch)), dma((n_ch,)), dma((n_ch,)),
            dma((12, 2)), dma((12, 2)), dma((2, slots)), dma((2, slots)),
        ],
        compiler_params=pltpu.CompilerParams(
            collective_id=0, has_side_effects=True, vmem_limit_bytes=60 * 1024 * 1024
        ),
    )(cond_x, cond_y, via_cond, via_mask, capacitance, pad_mask, observe)
    return pl.pallas_call(
        finish,
        out_shape=jax.ShapeDtypeStruct((2, 2, rows, cols), jnp.float32),
        in_specs=[pl.BlockSpec(memory_space=pltpu.VMEM)] * 4,
        out_specs=pl.BlockSpec(memory_space=pl.ANY),
        scratch_shapes=[block, dma((PIECES + 1,))],
        compiler_params=pltpu.CompilerParams(vmem_limit_bytes=8 * 1024 * 1024),
    )(*both)


def solution(mesh):
    placed = P("band", "tile", None)
    return jax.shard_map(
        on_device,
        mesh=mesh,
        in_specs=(placed,) * 6 + (P(None, "band", "tile", None),),
        out_specs=P(None, "band", "tile", None),
        check_vma=False,
    )
```
